32 devices in a mesh: groups: 2 (over y), slab: 16 (over z, x, core).
Axes of the slice: x: 2, y: 2, z: 4, core: 2. Of those that a mesh axis runs over, the one named last changes fastest.
Arguments:
- rhs: float32 [2, 64, 128, 128], P('groups', 'slab'), parts along dimension 0, may hold values from -6 to 6
- labels: int32 [64, 256, 128], P('slab', 'groups'), parts along dimension 1, may hold values from 0 to 4, as said below
- sigma_table: float32 [5, 3], replicated, may hold values from 0.05 to 2
Outputs:
- correction: float32 [2, 64, 128, 128], P('groups', 'slab'), parts along dimension 0
The draws below stay inside these ranges and needn't reach their ends.
There are 2 independent parts, one for each index of `groups`. The reference program is written for one: setup_inputs(seed, part) draws one part's arguments, and reference() takes and returns one part's arrays. A program takes and returns all parts, laid end to end along the dimension named above; an argument that names none is the same for every part. Nothing has to cross between parts.
Inputs may be any that keep to these rules, and one draw needn't show every extreme that they name: Label 0 marks exactly the voxels outside an ellipsoid centred on the grid with semi-axes 0.45 * 128, 0.45 * 128 and 0.55 * 64 cells; inside, labels 1 to 4 are drawn independently for each voxel.
All inputs are finite; a program needn't handle non-finite values.
Results may differ from the reference program's by a relative error of at most 0.0002.
Values sent between devices are 32-bit elements; how exact they have to be, the bound alone decides.
A program may use at most 64 MiB of HBM per device.

```python
import math
import jax
import jax.numpy as jnp
from jax import lax

R = 1
NX = 128
NY = 128
LABELS = 5
NZ = 64


def draw_labels(key, part):
    shape = (NZ, NX, NY)
    zcoord = lax.broadcasted_iota(jnp.int32, shape, 0)
    xcoord = lax.broadcasted_iota(jnp.int32, shape, 1)
    ycoord = lax.broadcasted_iota(jnp.int32, shape, 2)
    dist_z = 2 * zcoord + 1 - NZ
    dist_x = 2 * xcoord + 1 - NX
    dist_y = 2 * ycoord + 1 - NY
    term_x = 1000 * dist_x * dist_x // (81 * NX * NX // 100)
    term_y = 1000 * dist_y * dist_y // (81 * NY * NY // 100)
    term_z = 1000 * dist_z * dist_z // (121 * NZ * NZ // 100)
    inside = term_x + term_y + term_z < 1000
    tissue = jax.random.randint(jax.random.fold_in(key, 7), shape, 1, LABELS)
    return jnp.where(inside, tissue, 0).astype(jnp.int32)


def level_of(rng, dims, shards, smallest, high):
    def one(position, parts):
        steps = jax.random.uniform(jax.random.fold_in(jax.random.fold_in(rng, 6), position), (parts,), jnp.float32, smallest / len(shards), high / len(shards))
        return jnp.repeat(jnp.exp(steps), dims[position] // parts).reshape((-1,) + (1,) * (len(dims) - position - 1))

    factor_of = one(*shards[0])
    for cut in shards[1:]:
        factor_of = factor_of * one(*cut)
    return factor_of


def centred(key, dims, scale, bound, pieces=(), dtype=jnp.bfloat16):
    result = scale * jax.random.normal(key, dims, jnp.float32)
    if pieces:
        result = result * level_of(key, dims, pieces, -0.22, 0.18)
    return jnp.clip(result, -bound, bound).astype(dtype)


def setup_inputs(seed: int = 0, part: int = 0) -> dict:
    key_list = jax.random.split(jax.random.key(seed), 4)
    own_keys = jax.random.split(jax.random.fold_in(key_list[3], part), 4)
    return {
        "rhs": centred(own_keys[0], (R, NZ, NX, NY), 1.0, 6.0, ((1, 16),), jnp.float32),
        "labels": draw_labels(jax.random.fold_in(jax.random.fold_in(key_list[3], part), 71), part),
        "sigma_table": jnp.clip(jnp.exp(jax.random.uniform(key_list[2], (LABELS, 3), jnp.float32, math.log(0.05), math.log(2.0))), 0.05, 2.0),
    }


OMEGA = 0.8

def harmonic(lower_side, upper_side):
    return 2.0 * lower_side * upper_side / (lower_side + upper_side)

def conductivity(padded, sigma_table, column):
    running = jnp.zeros(padded.shape, jnp.float32)
    for tissue in range(LABELS):
        running = running + jnp.where(padded == tissue, sigma_table[tissue, column], 0.0)
    return running

def coefficients(labels_ext, sigma_table):
    padded = jnp.pad(labels_ext, ((0, 0), (1, 1), (1, 1)))
    active = (padded > 0).astype(jnp.float32)
    sigma_x = conductivity(padded, sigma_table, 0)
    sigma_y = conductivity(padded, sigma_table, 1)
    sigma_z = conductivity(padded, sigma_table, 2)
    inner_x = harmonic(sigma_x[1:-1, :-1, 1:-1], sigma_x[1:-1, 1:, 1:-1])
    couple_x = inner_x * active[1:-1, :-1, 1:-1] * active[1:-1, 1:, 1:-1]
    inner_y = harmonic(sigma_y[1:-1, 1:-1, :-1], sigma_y[1:-1, 1:-1, 1:])
    couple_y = inner_y * active[1:-1, 1:-1, :-1] * active[1:-1, 1:-1, 1:]
    inner_z = harmonic(sigma_z[:-1, 1:-1, 1:-1], sigma_z[1:, 1:-1, 1:-1])
    couple_z = inner_z * active[:-1, 1:-1, 1:-1] * active[1:, 1:-1, 1:-1]
    centre_mask = active[1:-1, 1:-1, 1:-1]
    faces = inner_x[:, :-1] + inner_x[:, 1:] + inner_y[:, :, :-1] + inner_y[:, :, 1:] + inner_z[:-1] + inner_z[1:]
    diagonal = centre_mask * faces + (1.0 - centre_mask)
    return (centre_mask, diagonal, couple_x, couple_y, couple_z)

def operate(extended, terms):
    couple_x, couple_y, couple_z = (terms[2], terms[3], terms[4])
    centre = extended[:, 1:-1]
    widened = jnp.pad(centre, ((0, 0), (0, 0), (1, 1), (1, 1)))
    neighbours = couple_x[:, :-1] * widened[:, :, :-2, 1:-1] + couple_x[:, 1:] * widened[:, :, 2:, 1:-1]
    neighbours = neighbours + couple_y[:, :, :-1] * widened[:, :, 1:-1, :-2] + couple_y[:, :, 1:] * widened[:, :, 1:-1, 2:]
    neighbours = neighbours + couple_z[:-1] * extended[:, :-2] + couple_z[1:] * extended[:, 2:]
    return terms[1] * centre - neighbours

def smooth(extended, source, terms):
    image = operate(extended, terms)
    return extended[:, 1:-1] + OMEGA * terms[0] * (source - image) / terms[1]

def start(source, terms):
    return OMEGA * terms[0] * source / terms[1]

def leftover(extended, source, terms):
    return terms[0] * (source - operate(extended, terms))

def pair_sum(values, along):
    even_part = [slice(None)] * values.ndim
    odd_part = [slice(None)] * values.ndim
    even_part[along] = slice(0, None, 2)
    odd_part[along] = slice(1, None, 2)
    return values[tuple(even_part)] + values[tuple(odd_part)]

def coarsen(terms):
    centre_mask, diagonal, couple_x, couple_y, couple_z = terms
    coarse_x = pair_sum(pair_sum(couple_x[:, 0::2], 0), 2)
    coarse_y = pair_sum(pair_sum(couple_y[:, :, 0::2], 0), 1)
    coarse_z = pair_sum(pair_sum(couple_z[0::2], 1), 2)
    internal = pair_sum(pair_sum(couple_x[:, 1::2], 0), 2) + pair_sum(pair_sum(couple_y[:, :, 1::2], 0), 1) + pair_sum(pair_sum(couple_z[1::2], 1), 2)
    counted = pair_sum(pair_sum(pair_sum(centre_mask, 0), 1), 2)
    raw_diag = pair_sum(pair_sum(pair_sum(centre_mask * diagonal, 0), 1), 2) - 2.0 * internal
    coarse_mask = jnp.minimum(counted, 1.0)
    coarse_diag = raw_diag + (1.0 - coarse_mask)
    return ((coarse_mask, coarse_diag, coarse_x, coarse_y, coarse_z), raw_diag)

def restrict(field):
    return pair_sum(pair_sum(pair_sum(field, 1), 2), 3)

def widen(field):
    return jnp.repeat(jnp.repeat(jnp.repeat(field, 2, axis=1), 2, axis=2), 2, axis=3)

def plane_total(values):
    return jnp.sum(values, axis=(-2, -1))

def line_terms(coarse_terms, raw_diag):
    line_diag = plane_total(raw_diag) - 2.0 * (plane_total(coarse_terms[2]) + plane_total(coarse_terms[3]))
    return (line_diag, plane_total(coarse_terms[4]))

def zeros_rim(field):
    return jnp.pad(field, ((0, 0), (1, 1), (0, 0), (0, 0)))

def reference(rhs, labels, sigma_table):
    padded_labels = jnp.pad(labels, ((1, 1), (0, 0), (0, 0)))
    fine_terms = coefficients(padded_labels, sigma_table)
    coarse_terms, raw_diag = coarsen(fine_terms)
    line_diag, line_faces = line_terms(coarse_terms, raw_diag)
    lower_band = -line_faces[:-1]
    upper_band = -line_faces[1:]

    def one_side(single):
        source = fine_terms[0] * single
        fine_first = start(source, fine_terms)
        fine_second = smooth(zeros_rim(fine_first), source, fine_terms)
        fine_left = leftover(zeros_rim(fine_second), source, fine_terms)
        coarse_source = restrict(fine_left)
        coarse_first = start(coarse_source, coarse_terms)
        coarse_second = smooth(zeros_rim(coarse_first), coarse_source, coarse_terms)
        coarse_left = leftover(zeros_rim(coarse_second), coarse_source, coarse_terms)
        line_rows = plane_total(coarse_left).T
        line_solution = lax.linalg.tridiagonal_solve(lower_band, line_diag, upper_band, line_rows)
        coarse_fix = coarse_second + coarse_terms[0] * line_solution.T[:, :, None, None]
        coarse_post = smooth(zeros_rim(coarse_fix), coarse_source, coarse_terms)
        coarse_final = smooth(zeros_rim(coarse_post), coarse_source, coarse_terms)
        fine_third = fine_second + fine_terms[0] * widen(coarse_final)
        fine_fourth = smooth(zeros_rim(fine_third), source, fine_terms)
        return smooth(zeros_rim(fine_fourth), source, fine_terms)
    return lax.map(one_side, rhs[:, None])[:, 0]
```

```python
import functools

import jax
import jax.numpy as jnp
from jax import lax
from jax.experimental import pallas as pl
from jax.experimental.pallas import tpu as pltpu
from jax.sharding import PartitionSpec as P

OMEGA = 0.8
LABELS = 5
MESH = pl.DeviceIdType.MESH


def copy_to(src, dst, sems, slot, target):
    return pltpu.make_async_remote_copy(
        src_ref=src,
        dst_ref=dst,
        send_sem=sems.at[0, slot],
        recv_sem=sems.at[1, slot],
        device_id={"slab": target},
        device_id_type=MESH,
    )


def kernel(
    n, rhs_hbm, lab_hbm, table, out_hbm,
    lab, rhs, gx, gxr, gy, gyr, gzl, gzh, idf, dg, ua, ub, tmp, pro,
    cof, d1, b1, vn, far_out, far_in, line_out, line_all, row_out, row_all, xs, outv,
    load_sem, sems, gather_sem,
):
    me = lax.axis_index("slab")
    nx, ny = lab.shape[1:]
    hx_rows = nx // 2
    has_low, has_up = me > 0, me < n - 1
    has_low2, has_up2 = me > 1, me < n - 2

    own_lab = pltpu.make_async_copy(lab_hbm, lab.at[pl.ds(3, 4)], load_sem.at[0])
    own_rhs = pltpu.make_async_copy(rhs_hbm.at[0], rhs.at[pl.ds(2, 4)], load_sem.at[1])
    own_lab.start()
    own_rhs.start()

    barrier = pltpu.get_barrier_semaphore()

    def greet(step, carry):
        other = lax.rem(me + step, n)
        pl.semaphore_signal(barrier, inc=1, device_id={"slab": other}, device_id_type=MESH)
        return carry

    lax.fori_loop(1, n, greet, 0)
    pl.semaphore_wait(barrier, n - 1)

    up, low = lax.rem(me + 1, n), lax.rem(me + n - 1, n)
    up2, low2 = lax.rem(me + 2, n), lax.rem(me + n - 2, n)

    lab_up = copy_to(lab_hbm.at[pl.ds(1, 3)], lab.at[pl.ds(0, 3)], sems, 0, up)
    lab_low = copy_to(lab_hbm.at[pl.ds(0, 3)], lab.at[pl.ds(7, 3)], sems, 1, low)
    rhs_up = copy_to(rhs_hbm.at[0, pl.ds(2, 2)], rhs.at[pl.ds(0, 2)], sems, 2, up)
    rhs_low = copy_to(rhs_hbm.at[0, pl.ds(0, 2)], rhs.at[pl.ds(6, 2)], sems, 3, low)
    cof_up = copy_to(cof.at[1], cof.at[0], sems, 4, up)
    cof_low = copy_to(cof.at[1], cof.at[2], sems, 5, low)
    b1_up = copy_to(b1.at[1], b1.at[0], sems, 6, up)
    b1_low = copy_to(b1.at[1], b1.at[2], sems, 7, low)
    u2_up = copy_to(ub.at[4], ub.at[0], sems, 8, up)
    u2_low = copy_to(ub.at[3], ub.at[7], sems, 9, low)
    vn_up = copy_to(vn.at[1], vn.at[0], sems, 10, up)
    vn_low = copy_to(vn.at[1], vn.at[2], sems, 11, low)
    far_up = copy_to(far_out.at[0], far_in.at[0], sems, 12, up2)
    far_low = copy_to(far_out.at[1], far_in.at[1], sems, 13, low2)

    def send(upward, downward):
        pl.when(has_up)(upward.start)
        pl.when(has_low)(downward.start)

    def receive(upward, downward):
        pl.when(has_low)(upward.wait_recv)
        pl.when(has_up)(downward.wait_recv)

    send(lab_up, lab_low)
    send(rhs_up, rhs_low)

    def clear(ref, first, count):
        for k in range(first, first + count):
            ref[k] = jnp.zeros(ref.shape[1:], ref.dtype)

    @pl.when(me == 0)
    def _():
        clear(lab, 0, 3)
        clear(rhs, 0, 2)
        clear(cof.at[0], 0, 5)
        clear(b1, 0, 1)
        clear(ub, 0, 1)
        clear(vn, 0, 1)

    @pl.when(me == n - 1)
    def _():
        clear(lab, 7, 3)
        clear(rhs, 6, 2)
        clear(cof.at[2], 0, 5)
        clear(b1, 2, 1)
        clear(ub, 7, 1)
        clear(vn, 2, 1)

    @pl.when(me < 2)
    def _():
        clear(far_in, 0, 1)

    @pl.when(me >= n - 2)
    def _():
        clear(far_in, 1, 1)

    xs[...] = jnp.zeros(xs.shape, xs.dtype)

    fine_row = lax.broadcasted_iota(jnp.int32, (nx, ny), 0) % 2 == 1
    fine_lane = lax.broadcasted_iota(jnp.int32, (nx, ny), 1) % 2 == 1
    even = lax.broadcasted_iota(jnp.int32, (hx_rows, ny), 1) % 2 == 0

    def select(values, column):
        chosen = jnp.full(values.shape, table[0, column], jnp.float32)
        for tissue in range(1, LABELS):
            chosen = jnp.where(values == tissue, table[tissue, column], chosen)
        return chosen

    def harmonic(a, b):
        return 2.0 * a * b / (a + b)

    def plane_terms(k):
        here, below, above = lab[k + 1], lab[k], lab[k + 2]
        a = (here > 0).astype(jnp.float32)
        sx, sy, sz = select(here, 0), select(here, 1), select(here, 2)
        hx = harmonic(pltpu.roll(sx, 1, 0), sx)
        faces = hx + pltpu.roll(hx, nx - 1, 0)
        cx = hx * a * pltpu.roll(a, 1, 0)
        gx[k] = cx
        gxr[k] = pltpu.roll(cx, nx - 1, 0)
        hy = harmonic(pltpu.roll(sy, 1, 1), sy)
        faces = faces + hy + pltpu.roll(hy, ny - 1, 1)
        cy = hy * a * pltpu.roll(a, 1, 1)
        gy[k] = cy
        gyr[k] = pltpu.roll(cy, ny - 1, 1)
        hl = harmonic(select(below, 2), sz)
        gzl[k] = hl * a * (below > 0).astype(jnp.float32)
        hh = harmonic(sz, select(above, 2))
        gzh[k] = hh * a * (above > 0).astype(jnp.float32)
        faces = faces + hl + hh
        diagonal = a * faces + (1.0 - a)
        dg[k] = diagonal
        idf[k] = OMEGA * a / diagonal

    def over(first, last, body):
        def step(k, carry):
            body(k)
            return carry

        lax.fori_loop(first, last, step, 0)

    own_lab.wait()
    receive(lab_up, lab_low)
    over(0, 8, plane_terms)

    def rows_even(plane):
        tmp[0] = plane
        return tmp[0, pl.ds(0, hx_rows, 2), :]

    def rows_sum(plane):
        tmp[0] = plane
        return tmp[0, pl.ds(0, hx_rows, 2), :] + tmp[0, pl.ds(1, hx_rows, 2), :]

    def lanes_sum(t0, t1):
        return jnp.where(even, t0 + pltpu.roll(t0, ny - 1, 1), t1 + pltpu.roll(t1, 1, 1))

    def lanes_even(t0, t1):
        return jnp.where(even, t0, pltpu.roll(t1, 1, 1))

    def restrict(p0, p1):
        return lanes_sum(rows_sum(p0), rows_sum(p1))

    def inner(k):
        mask = (idf[k] > 0.0).astype(jnp.float32)
        doubled = jnp.where(fine_row, gx[k], 0.0) + jnp.where(fine_lane, gy[k], 0.0)
        if k % 2 == 1:
            doubled = doubled + gzl[k]
        return mask * dg[k] - 2.0 * doubled, mask

    (f0, m0), (f1, m1), (f2, m2), (f3, m3) = inner(2), inner(3), inner(4), inner(5)
    raw = restrict(f0 + f1, f2 + f3)
    active1 = jnp.minimum(restrict(m0 + m1, m2 + m3), 1.0)
    diag1 = raw + (1.0 - active1)
    d1[...] = diag1
    cof[1, 0] = OMEGA * active1 / diag1
    coarse_x = lanes_sum(rows_even(gx[2] + gx[3]), rows_even(gx[4] + gx[5]))
    coarse_y = lanes_even(rows_sum(gy[2] + gy[3]), rows_sum(gy[4] + gy[5]))
    coarse_zl = restrict(gzl[2], gzl[4])
    cof[1, 1] = coarse_x
    cof[1, 2] = coarse_y
    cof[1, 3] = coarse_zl
    cof[1, 4] = restrict(gzh[3], gzh[5])
    send(cof_up, cof_low)

    def plane_sums(packed):
        lower = jnp.sum(jnp.where(even, packed, 0.0), axis=0, keepdims=True)
        upper = jnp.sum(jnp.where(even, 0.0, packed), axis=0, keepdims=True)
        lower = jnp.sum(lower, axis=1, keepdims=True)
        upper = jnp.sum(upper, axis=1, keepdims=True)
        return lower, upper

    sub = lax.broadcasted_iota(jnp.int32, (8, ny), 0)

    def gather(out, everyone, slot, values):
        tile = jnp.zeros((8, ny), jnp.float32)
        for row, value in enumerate(values):
            tile = jnp.where(sub == row, value, tile)
        out[...] = tile
        everyone[me] = tile

        def one(step, carry):
            pltpu.make_async_remote_copy(
                src_ref=out,
                dst_ref=everyone.at[me],
                send_sem=gather_sem.at[0, slot],
                recv_sem=gather_sem.at[1, slot],
                device_id={"slab": lax.rem(me + step, n)},
                device_id_type=MESH,
            ).start()
            return carry

        lax.fori_loop(1, n, one, 0)

    def gather_wait(everyone, side, slot):
        rest = everyone.at[pl.ds(0, n - 1)]
        pltpu.make_async_copy(rest, rest, gather_sem.at[side, slot]).wait()

    dl, du = plane_sums(raw - 2.0 * (coarse_x + coarse_y))
    fl, fu = plane_sums(coarse_zl)
    gather(line_out, line_all, 0, (dl, du, fl, fu))

    own_rhs.wait()
    receive(rhs_up, rhs_low)

    def first_sweep(k):
        ua[k] = idf[k] * rhs[k]

    over(0, 8, first_sweep)

    def neighbours(field, k):
        u = field[k]
        total = gx[k] * pltpu.roll(u, 1, 0) + gxr[k] * pltpu.roll(u, nx - 1, 0)
        total = total + gy[k] * pltpu.roll(u, 1, 1) + gyr[k] * pltpu.roll(u, ny - 1, 1)
        return u, total + gzl[k] * field[k - 1] + gzh[k] * field[k + 1]

    def sweep(src, dst, shift=0):
        def body(k):
            u, total = neighbours(src, k)
            dst[k - shift] = (1.0 - OMEGA) * u + idf[k] * (rhs[k] + total)

        return body

    over(1, 7, sweep(ua, ub))

    def residual(k):
        u, total = neighbours(ub, k)
        return jnp.where(idf[k] > 0.0, rhs[k] - dg[k] * u + total, 0.0)

    b1[1] = restrict(residual(2) + residual(3), residual(4) + residual(5))
    send(b1_up, b1_low)

    gather_wait(line_all, 1, 0)
    flat = line_all.reshape(n * 8, ny)

    def line_rows(ref, row):
        return ref[pl.ds(row, n, 8), :]

    de, do, fe, fo = (line_rows(flat, row) for row in range(4))

    def back(x, s):
        return pltpu.roll(x, s % n, 0)

    def ahead(x, s):
        return pltpu.roll(x, (n - s) % n, 0)

    inv_odd = 1.0 / do
    to_low = fe * back(inv_odd, 1)
    to_up = fo * inv_odd
    fe_next = ahead(fe, 1)
    diag = de - fe * to_low - fo * to_up
    lower = -to_low * back(fo, 1)
    upper = -to_up * fe_next
    steps = []
    shift = 1
    while shift < n:
        alpha, gamma = lower / back(diag, shift), upper / ahead(diag, shift)
        steps.append((shift, alpha, gamma))
        diag = diag - alpha * back(upper, shift) - gamma * ahead(lower, shift)
        lower, upper = -alpha * back(lower, shift), -gamma * ahead(upper, shift)
        shift *= 2
    inv_diag = 1.0 / diag

    receive(cof_up, cof_low)
    receive(b1_up, b1_low)
    send(u2_up, u2_low)

    zero = jnp.zeros((hx_rows, ny), jnp.float32)

    def coarse_neighbours(k, below, f, above):
        cx, cy = cof[k, 1], cof[k, 2]
        zl = jnp.where(even, pltpu.roll(below, ny - 1, 1), pltpu.roll(f, 1, 1))
        zh = jnp.where(even, pltpu.roll(f, ny - 1, 1), pltpu.roll(above, 1, 1))
        total = cx * pltpu.roll(f, 1, 0)
        total = total + pltpu.roll(cx, hx_rows - 1, 0) * pltpu.roll(f, hx_rows - 1, 0)
        total = total + cy * pltpu.roll(f, 2, 1)
        total = total + pltpu.roll(cy, ny - 2, 1) * pltpu.roll(f, ny - 2, 1)
        return total + cof[k, 3] * zl + cof[k, 4] * zh

    def coarse_sweep(fields):
        swept = []
        for k in range(3):
            total = coarse_neighbours(k, fields[k], fields[k + 1], fields[k + 2])
            swept.append((1.0 - OMEGA) * fields[k + 1] + cof[k, 0] * (b1[k] + total))
        return [zero] + swept + [zero]

    v1 = [zero] + [cof[k, 0] * b1[k] for k in range(3)] + [zero]
    v2 = coarse_sweep(v1)
    own_total = coarse_neighbours(1, v2[1], v2[2], v2[3])
    r1 = jnp.where(cof[1, 0] > 0.0, b1[1] - d1[...] * v2[2] + own_total, 0.0)
    gather(row_out, row_all, 1, plane_sums(r1))
    vn[1] = v2[2]
    far_out[0] = jnp.where(even, pltpu.roll(cof[1, 0], ny - 1, 1), v2[2])
    far_out[1] = jnp.where(even, v2[2], pltpu.roll(cof[1, 0], 1, 1))
    send(vn_up, vn_low)
    pl.when(has_up2)(far_up.start)
    pl.when(has_low2)(far_low.start)

    gather_wait(row_all, 1, 1)
    flat_rows = row_all.reshape(n * 8, ny)
    be, bo = line_rows(flat_rows, 0), line_rows(flat_rows, 1)
    reduced = be + to_low * back(bo, 1) + to_up * bo
    for shift, alpha, gamma in steps:
        reduced = reduced - alpha * back(reduced, shift) - gamma * ahead(reduced, shift)
    e_even = reduced * inv_diag
    e_odd = (bo + fo * e_even + fe_next * ahead(e_even, 1)) * inv_odd
    line_even = lax.broadcasted_iota(jnp.int32, (n, ny), 1) % 2 == 0
    xs[pl.ds(8, n), :] = jnp.where(line_even, e_even, e_odd)

    def line(k):
        return jnp.broadcast_to(xs[pl.ds(me + 8 + k, 1), :], (hx_rows, ny))

    receive(vn_up, vn_low)
    pl.when(has_low2)(far_up.wait_recv)
    pl.when(has_up2)(far_low.wait_recv)
    far_below, far_above = far_in[0], far_in[1]
    w1 = [far_below + jnp.where(pltpu.roll(far_below, 1, 1) > 0.0, line(-2), 0.0)]
    for k in range(3):
        w1.append(vn[k] + jnp.where(cof[k, 0] > 0.0, line(k - 1), 0.0))
    w1.append(far_above + jnp.where(pltpu.roll(far_above, ny - 1, 1) > 0.0, line(2), 0.0))
    w3 = coarse_sweep(coarse_sweep(w1))

    def prolong(slot, plane):
        pro[slot, pl.ds(0, hx_rows, 2), :] = plane
        pro[slot, pl.ds(1, hx_rows, 2), :] = plane

    def lower_plane(pack):
        return jnp.where(even, pack, pltpu.roll(pack, 1, 1))

    def upper_plane(pack):
        return jnp.where(even, pltpu.roll(pack, ny - 1, 1), pack)

    prolong(0, upper_plane(w3[1]))
    prolong(1, lower_plane(w3[2]))
    prolong(2, upper_plane(w3[2]))
    prolong(3, lower_plane(w3[3]))

    receive(u2_up, u2_low)

    def correct(k):
        ua[k] = ub[k] + jnp.where(idf[k] > 0.0, pro[k // 2], 0.0)

    over(0, 8, correct)

    pl.when(has_up)(u2_up.wait_send)
    pl.when(has_low)(u2_low.wait_send)
    over(1, 7, sweep(ua, tmp))
    over(2, 6, sweep(tmp, outv, 2))
    store = pltpu.make_async_copy(outv, out_hbm.at[0], load_sem.at[2])
    store.start()

    for upward, downward in (
        (lab_up, lab_low), (rhs_up, rhs_low), (cof_up, cof_low), (b1_up, b1_low), (vn_up, vn_low),
    ):
        pl.when(has_up)(upward.wait_send)
        pl.when(has_low)(downward.wait_send)
    pl.when(has_up2)(far_up.wait_send)
    pl.when(has_low2)(far_low.wait_send)
    gather_wait(line_all, 0, 0)
    gather_wait(row_all, 0, 1)
    store.wait()


def on_device(n, rhs, labels, sigma_table):
    planes, nx, ny = labels.shape
    fine = lambda count: pltpu.VMEM((count, nx, ny), jnp.float32)
    packs = lambda *counts: pltpu.VMEM((*counts, nx // 2, ny), jnp.float32)
    tiles = lambda *counts: pltpu.VMEM((*counts, 8, ny), jnp.float32)
    return pl.pallas_call(
        functools.partial(kernel, n),
        out_shape=jax.ShapeDtypeStruct(rhs.shape, jnp.float32),
        in_specs=[
            pl.BlockSpec(memory_space=pl.ANY),
            pl.BlockSpec(memory_space=pl.ANY),
            pl.BlockSpec(memory_space=pltpu.SMEM),
        ],
        out_specs=pl.BlockSpec(memory_space=pl.ANY),
        scratch_shapes=[
            pltpu.VMEM((10, nx, ny), jnp.int32),
            fine(8), fine(8), fine(8), fine(8), fine(8), fine(8), fine(8), fine(8), fine(8),
            fine(8), fine(8), fine(8), fine(4),
            packs(3, 5), packs(), packs(3), packs(3), packs(2), packs(2),
            tiles(), tiles(n), tiles(), tiles(n),
            pltpu.VMEM((n + 16, ny), jnp.float32),
            fine(4),
            pltpu.SemaphoreType.DMA((3,)),
            pltpu.SemaphoreType.DMA((2, 14)),
            pltpu.SemaphoreType.DMA((2, 2)),
        ],
        compiler_params=pltpu.CompilerParams(collective_id=0, has_side_effects=True),
    )(rhs, labels, sigma_table)


def solution(mesh):
    placed = (P("groups", "slab", None, None), P("slab", "groups", None), P())
    return jax.shard_map(
        functools.partial(on_device, mesh.shape["slab"]),
        mesh=mesh,
        in_specs=placed,
        out_specs=P("groups", "slab", None, None),
        check_vma=False,
    )
```

```python
import functools

import jax
import jax.numpy as jnp
from jax import lax
from jax.experimental import pallas as pl
from jax.experimental.pallas import tpu as pltpu
from jax.sharding import PartitionSpec as P

OMEGA = 0.8
LABELS = 5
MESH = pl.DeviceIdType.MESH


def copy_to(src, dst, sems, slot, target):
    return pltpu.make_async_remote_copy(
        src_ref=src,
        dst_ref=dst,
        send_sem=sems.at[0, slot],
        recv_sem=sems.at[1, slot],
        device_id={"slab": target},
        device_id_type=MESH,
    )


def kernel(
    n, rhs_hbm, lab_hbm, table_hbm, out_hbm,
    lab, rhs, gx, gxr, gy, gyr, gzl, gzh, idf, dg, ua, ub, tmp, pro,
    cof, d1, b1, vn, line_out, line_all, row_out, row_all, xs, outv, table,
    load_sem, sems, gather_sem,
):
    me = lax.axis_index("slab")
    nx, ny = lab.shape[1:]
    hx_rows = nx // 2
    has_low, has_up = me > 0, me < n - 1

    load_table = pltpu.make_async_copy(table_hbm, table, load_sem.at[3])
    load_table.start()
    barrier = pltpu.get_barrier_semaphore()

    def greet(step, carry):
        other = lax.rem(me + step, n)
        pl.semaphore_signal(barrier, inc=1, device_id={"slab": other}, device_id_type=MESH)
        return carry

    lax.fori_loop(1, n, greet, 0)
    pl.semaphore_wait(barrier, n - 1)

    up, low = lax.rem(me + 1, n), lax.rem(me + n - 1, n)
    near_up = copy_to(lab_hbm.at[3], lab.at[1], sems, 0, up)
    near_low = copy_to(lab_hbm.at[0], lab.at[6], sems, 1, low)
    next_up = copy_to(lab_hbm.at[2], lab.at[0], sems, 2, up)
    next_low = copy_to(lab_hbm.at[1], lab.at[7], sems, 3, low)
    rhs_up = copy_to(rhs_hbm.at[0, 3], rhs.at[1], sems, 4, up)
    rhs_low = copy_to(rhs_hbm.at[0, 0], rhs.at[6], sems, 5, low)
    u1_up = copy_to(ua.at[4], ua.at[0], sems, 6, up)
    u1_low = copy_to(ua.at[3], ua.at[7], sems, 7, low)
    cof_up = copy_to(cof.at[1, pl.ds(0, 4)], cof.at[0, pl.ds(0, 4)], sems, 8, up)
    cof_low = copy_to(cof.at[1, pl.ds(1, 4)], cof.at[2, pl.ds(1, 4)], sems, 9, low)
    b1_up = copy_to(b1.at[1], b1.at[0], sems, 10, up)
    b1_low = copy_to(b1.at[1], b1.at[2], sems, 11, low)
    u2_up = copy_to(ub.at[4], ub.at[0], sems, 12, up)
    u2_low = copy_to(ub.at[3], ub.at[7], sems, 13, low)
    vn_up = copy_to(vn.at[1], vn.at[0], sems, 14, up)
    vn_low = copy_to(vn.at[1], vn.at[2], sems, 15, low)

    def send(upward, downward):
        pl.when(has_up)(upward.start)
        pl.when(has_low)(downward.start)

    def receive(upward, downward):
        pl.when(has_low)(upward.wait_recv)
        pl.when(has_up)(downward.wait_recv)

    send(near_up, near_low)
    own_lab = pltpu.make_async_copy(lab_hbm, lab.at[pl.ds(2, 4)], load_sem.at[0])
    own_rhs = pltpu.make_async_copy(rhs_hbm.at[0], rhs.at[pl.ds(2, 4)], load_sem.at[1])
    own_lab.start()
    own_rhs.start()
    send(next_up, next_low)
    send(rhs_up, rhs_low)

    def clear(ref, first, count):
        for k in range(first, first + count):
            ref[k] = jnp.zeros(ref.shape[1:], ref.dtype)

    @pl.when(me == 0)
    def _():
        clear(lab, 0, 2)
        clear(rhs, 1, 1)
        clear(ua, 0, 1)
        clear(cof.at[0], 0, 4)
        clear(b1, 0, 1)
        clear(ub, 0, 1)
        clear(vn, 0, 1)

    @pl.when(me == n - 1)
    def _():
        clear(lab, 6, 2)
        clear(rhs, 6, 1)
        clear(ua, 7, 1)
        clear(cof.at[2], 1, 4)
        clear(b1, 2, 1)
        clear(ub, 7, 1)
        clear(vn, 2, 1)

    xs[...] = jnp.zeros(xs.shape, xs.dtype)

    fine_row = lax.broadcasted_iota(jnp.int32, (nx, ny), 0) % 2 == 1
    fine_lane = lax.broadcasted_iota(jnp.int32, (nx, ny), 1) % 2 == 1
    even = lax.broadcasted_iota(jnp.int32, (hx_rows, ny), 1) % 2 == 0

    def select(values, column):
        chosen = jnp.full(values.shape, table[column, 0], jnp.float32)
        for tissue in range(1, LABELS):
            chosen = jnp.where(values == tissue, table[column, tissue], chosen)
        return chosen

    def harmonic(a, b):
        return 2.0 * a * b / (a + b)

    def plane_terms(k):
        here, below, above = lab[k], lab[k - 1], lab[k + 1]
        a = (here > 0).astype(jnp.float32)
        sx, sy, sz = select(here, 0), select(here, 1), select(here, 2)
        hx = harmonic(pltpu.roll(sx, 1, 0), sx)
        faces = hx + pltpu.roll(hx, nx - 1, 0)
        cx = hx * a * pltpu.roll(a, 1, 0)
        gx[k] = cx
        gxr[k] = pltpu.roll(cx, nx - 1, 0)
        hy = harmonic(pltpu.roll(sy, 1, 1), sy)
        faces = faces + hy + pltpu.roll(hy, ny - 1, 1)
        cy = hy * a * pltpu.roll(a, 1, 1)
        gy[k] = cy
        gyr[k] = pltpu.roll(cy, ny - 1, 1)
        hl = harmonic(select(below, 2), sz)
        gzl[k] = hl * a * (below > 0).astype(jnp.float32)
        hh = harmonic(sz, select(above, 2))
        gzh[k] = hh * a * (above > 0).astype(jnp.float32)
        faces = faces + hl + hh
        diagonal = a * faces + (1.0 - a)
        dg[k] = diagonal
        idf[k] = OMEGA * a / diagonal

    def over(first, last, body):
        def step(k, carry):
            body(k)
            return carry

        lax.fori_loop(first, last, step, 0)

    def first_sweep(k):
        ua[k] = idf[k] * rhs[k]

    load_table.wait()
    own_lab.wait()
    over(3, 5, plane_terms)
    own_rhs.wait()
    over(3, 5, first_sweep)
    send(u1_up, u1_low)

    receive(near_up, near_low)
    over(0, 2, lambda k: plane_terms(2 + 3 * k))
    over(0, 2, lambda k: first_sweep(2 + 3 * k))

    def rows_even(plane):
        tmp[0] = plane
        return tmp[0, pl.ds(0, hx_rows, 2), :]

    def rows_sum(plane):
        tmp[0] = plane
        return tmp[0, pl.ds(0, hx_rows, 2), :] + tmp[0, pl.ds(1, hx_rows, 2), :]

    def lanes_sum(t0, t1):
        return jnp.where(even, t0 + pltpu.roll(t0, ny - 1, 1), t1 + pltpu.roll(t1, 1, 1))

    def lanes_even(t0, t1):
        return jnp.where(even, t0, pltpu.roll(t1, 1, 1))

    def restrict(p0, p1):
        return lanes_sum(rows_sum(p0), rows_sum(p1))

    def inner(k):
        mask = (idf[k] > 0.0).astype(jnp.float32)
        doubled = jnp.where(fine_row, gx[k], 0.0) + jnp.where(fine_lane, gy[k], 0.0)
        if k % 2 == 1:
            doubled = doubled + gzl[k]
        return mask * dg[k] - 2.0 * doubled, mask

    (f0, m0), (f1, m1), (f2, m2), (f3, m3) = inner(2), inner(3), inner(4), inner(5)
    raw = restrict(f0 + f1, f2 + f3)
    active1 = jnp.minimum(restrict(m0 + m1, m2 + m3), 1.0)
    diag1 = raw + (1.0 - active1)
    d1[...] = diag1
    cof[1, 1] = OMEGA * active1 / diag1
    coarse_x = lanes_sum(rows_even(gx[2] + gx[3]), rows_even(gx[4] + gx[5]))
    coarse_y = lanes_even(rows_sum(gy[2] + gy[3]), rows_sum(gy[4] + gy[5]))
    coarse_zl = restrict(gzl[2], gzl[4])
    cof[1, 2] = coarse_x
    cof[1, 3] = coarse_y
    cof[1, 0] = coarse_zl
    cof[1, 4] = restrict(gzh[3], gzh[5])
    send(cof_up, cof_low)

    def plane_sums(packed):
        lower = jnp.sum(jnp.where(even, packed, 0.0), axis=0, keepdims=True)
        upper = jnp.sum(jnp.where(even, 0.0, packed), axis=0, keepdims=True)
        lower = jnp.sum(lower, axis=1, keepdims=True)
        upper = jnp.sum(upper, axis=1, keepdims=True)
        return lower, upper

    sub = lax.broadcasted_iota(jnp.int32, (8, ny), 0)

    sub_even = lax.broadcasted_iota(jnp.int32, (8, ny), 1) % 2 == 0

    def gather(out, everyone, slot, pairs):
        tile = jnp.zeros((8, ny), jnp.float32)
        for row, (lower, upper) in enumerate(pairs):
            tile = jnp.where(sub == row, jnp.where(sub_even, lower, upper), tile)
        out[...] = tile
        everyone[me] = tile
        rows = pl.ds(0, len(pairs))

        def one(step, carry):
            pltpu.make_async_remote_copy(
                src_ref=out.at[rows],
                dst_ref=everyone.at[me, rows],
                send_sem=gather_sem.at[0, slot],
                recv_sem=gather_sem.at[1, slot],
                device_id={"slab": lax.rem(me + step, n)},
                device_id_type=MESH,
            ).start()
            return carry

        lax.fori_loop(1, n, one, 0)

    def gather_wait(everyone, side, slot, count):
        rest = everyone.at[pl.ds(0, n - 1), pl.ds(0, count)]
        pltpu.make_async_copy(rest, rest, gather_sem.at[side, slot]).wait()

    line_diag = plane_sums(raw - 2.0 * (coarse_x + coarse_y))
    gather(line_out, line_all, 0, (line_diag, plane_sums(coarse_zl)))

    receive(next_up, next_low)
    over(0, 2, lambda k: plane_terms(1 + 5 * k))
    receive(rhs_up, rhs_low)
    over(0, 2, lambda k: first_sweep(1 + 5 * k))
    receive(u1_up, u1_low)

    def neighbours(field, k):
        u = field[k]
        total = gx[k] * pltpu.roll(u, 1, 0) + gxr[k] * pltpu.roll(u, nx - 1, 0)
        total = total + gy[k] * pltpu.roll(u, 1, 1) + gyr[k] * pltpu.roll(u, ny - 1, 1)
        return u, total + gzl[k] * field[k - 1] + gzh[k] * field[k + 1]

    def sweep(src, dst, shift=0):
        def body(k):
            u, total = neighbours(src, k)
            dst[k - shift] = (1.0 - OMEGA) * u + idf[k] * (rhs[k] + total)

        return body

    over(1, 7, sweep(ua, ub))

    def residual(k):
        u, total = neighbours(ub, k)
        return jnp.where(idf[k] > 0.0, rhs[k] - dg[k] * u + total, 0.0)

    b1[1] = restrict(residual(2) + residual(3), residual(4) + residual(5))
    send(b1_up, b1_low)
    send(u2_up, u2_low)

    gather_wait(line_all, 1, 0, 2)

    line_even = lax.broadcasted_iota(jnp.int32, (n, ny), 1) % 2 == 0

    def line_rows(everyone, row):
        both = everyone.reshape(n * 8, ny)[pl.ds(row, n, 8), :]
        lower = jnp.where(line_even, both, pltpu.roll(both, 1, 1))
        return lower, jnp.where(line_even, pltpu.roll(both, ny - 1, 1), both)

    (de, do), (fe, fo) = line_rows(line_all, 0), line_rows(line_all, 1)

    def back(x, s):
        return pltpu.roll(x, s % n, 0)

    def ahead(x, s):
        return pltpu.roll(x, (n - s) % n, 0)

    inv_odd = 1.0 / do
    to_low = fe * back(inv_odd, 1)
    to_up = fo * inv_odd
    fe_next = ahead(fe, 1)
    diag = de - fe * to_low - fo * to_up
    lower = -to_low * back(fo, 1)
    upper = -to_up * fe_next
    steps = []
    shift = 1
    while shift < n:
        alpha, gamma = lower / back(diag, shift), upper / ahead(diag, shift)
        steps.append((shift, alpha, gamma))
        diag = diag - alpha * back(upper, shift) - gamma * ahead(lower, shift)
        lower, upper = -alpha * back(lower, shift), -gamma * ahead(upper, shift)
        shift *= 2
    inv_diag = 1.0 / diag

    receive(cof_up, cof_low)
    cof[0, 4] = jnp.where(even, pltpu.roll(cof[0, 0], ny - 1, 1), pltpu.roll(cof[1, 0], 1, 1))
    cof[2, 0] = jnp.where(even, pltpu.roll(cof[1, 4], ny - 1, 1), pltpu.roll(cof[2, 4], 1, 1))
    receive(b1_up, b1_low)

    zero = jnp.zeros((hx_rows, ny), jnp.float32)

    def coarse_neighbours(k, below, f, above):
        cx, cy = cof[k, 2], cof[k, 3]
        zl = jnp.where(even, pltpu.roll(below, ny - 1, 1), pltpu.roll(f, 1, 1))
        zh = jnp.where(even, pltpu.roll(f, ny - 1, 1), pltpu.roll(above, 1, 1))
        total = cx * pltpu.roll(f, 1, 0)
        total = total + pltpu.roll(cx, hx_rows - 1, 0) * pltpu.roll(f, hx_rows - 1, 0)
        total = total + cy * pltpu.roll(f, 2, 1)
        total = total + pltpu.roll(cy, ny - 2, 1) * pltpu.roll(f, ny - 2, 1)
        return total + cof[k, 0] * zl + cof[k, 4] * zh

    def coarse_sweep(fields):
        swept = []
        for k in range(3):
            total = coarse_neighbours(k, fields[k], fields[k + 1], fields[k + 2])
            swept.append((1.0 - OMEGA) * fields[k + 1] + cof[k, 1] * (b1[k] + total))
        return [zero] + swept + [zero]

    v1 = [zero] + [cof[k, 1] * b1[k] for k in range(3)] + [zero]
    v2 = coarse_sweep(v1)
    own_total = coarse_neighbours(1, v2[1], v2[2], v2[3])
    r1 = jnp.where(cof[1, 1] > 0.0, b1[1] - d1[...] * v2[2] + own_total, 0.0)
    gather(row_out, row_all, 1, (plane_sums(r1),))
    vn[1] = (1.0 - OMEGA) * v2[2] + cof[1, 1] * (b1[1] + own_total)
    send(vn_up, vn_low)

    parts = []
    for k in range(3):
        weight, cx, cy = cof[k, 1], cof[k, 2], cof[k, 3]
        around = cx + pltpu.roll(cx, hx_rows - 1, 0) + cy + pltpu.roll(cy, ny - 2, 1)
        own_part = jnp.where(weight > 0.0, 1.0 - OMEGA, 0.0) + weight * around
        parts.append((own_part, weight * cof[k, 0], weight * cof[k, 4]))
    receive(vn_up, vn_low)

    gather_wait(row_all, 1, 1, 1)
    be, bo = line_rows(row_all, 0)
    reduced = be + to_low * back(bo, 1) + to_up * bo
    for shift, alpha, gamma in steps:
        reduced = reduced - alpha * back(reduced, shift) - gamma * ahead(reduced, shift)
    e_even = reduced * inv_diag
    e_odd = (bo + fo * e_even + fe_next * ahead(e_even, 1)) * inv_odd
    packed = jnp.where(line_even, e_even, e_odd)
    xs[0, pl.ds(8, n), :] = packed
    xs[1, pl.ds(8, n), :] = jnp.where(line_even, back(e_odd, 1), e_even)
    xs[2, pl.ds(8, n), :] = jnp.where(line_even, e_odd, ahead(e_even, 1))

    def line(slot, k):
        return jnp.broadcast_to(xs[slot, pl.ds(me + 7 + k, 1), :], (hx_rows, ny))

    w2 = [zero]
    for k, (own_part, lower_part, upper_part) in enumerate(parts):
        fixed = own_part * line(0, k) + lower_part * line(1, k) + upper_part * line(2, k)
        w2.append(vn[k] + fixed)
    w3 = coarse_sweep(w2 + [zero])

    def prolong(slot, plane):
        pro[slot, pl.ds(0, hx_rows, 2), :] = plane
        pro[slot, pl.ds(1, hx_rows, 2), :] = plane

    def lower_plane(pack):
        return jnp.where(even, pack, pltpu.roll(pack, 1, 1))

    def upper_plane(pack):
        return jnp.where(even, pltpu.roll(pack, ny - 1, 1), pack)

    prolong(0, upper_plane(w3[1]))
    prolong(1, lower_plane(w3[2]))
    prolong(2, upper_plane(w3[2]))
    prolong(3, lower_plane(w3[3]))

    receive(u2_up, u2_low)

    def correct(k):
        ua[k] = ub[k] + jnp.where(lab[k] > 0, pro[k // 2], 0.0)

    pl.when(has_up)(u1_up.wait_send)
    pl.when(has_low)(u1_low.wait_send)
    over(0, 8, correct)

    over(1, 7, sweep(ua, tmp))
    over(2, 6, sweep(tmp, outv, 2))
    store = pltpu.make_async_copy(outv, out_hbm.at[0], load_sem.at[2])
    store.start()

    for upward, downward in (
        (near_up, near_low), (next_up, next_low), (rhs_up, rhs_low), (cof_up, cof_low), (b1_up, b1_low), (vn_up, vn_low),
        (u2_up, u2_low),
    ):
        pl.when(has_up)(upward.wait_send)
        pl.when(has_low)(downward.wait_send)
    gather_wait(line_all, 0, 0, 2)
    gather_wait(row_all, 0, 1, 1)
    store.wait()


def on_device(n, rhs, labels, sigma_table):
    planes, nx, ny = labels.shape
    fine = lambda count: pltpu.VMEM((count, nx, ny), jnp.float32)
    packs = lambda *counts: pltpu.VMEM((*counts, nx // 2, ny), jnp.float32)
    tiles = lambda *counts: pltpu.VMEM((*counts, 8, ny), jnp.float32)
    return pl.pallas_call(
        functools.partial(kernel, n),
        out_shape=jax.ShapeDtypeStruct(rhs.shape, jnp.float32),
        in_specs=[
            pl.BlockSpec(memory_space=pl.ANY),
            pl.BlockSpec(memory_space=pl.ANY),
            pl.BlockSpec(memory_space=pl.ANY),
        ],
        out_specs=pl.BlockSpec(memory_space=pl.ANY),
        scratch_shapes=[
            pltpu.VMEM((8, nx, ny), jnp.int32),
            fine(8), fine(8), fine(8), fine(8), fine(8), fine(8), fine(8), fine(8), fine(8),
            fine(8), fine(8), fine(8), fine(4),
            packs(3, 5), packs(), packs(3), packs(3),
            tiles(), tiles(n), tiles(), tiles(n),
            pltpu.VMEM((3, n + 16, ny), jnp.float32),
            fine(4),
            pltpu.SMEM((3, LABELS), jnp.float32),
            pltpu.SemaphoreType.DMA((4,)),
            pltpu.SemaphoreType.DMA((2, 16)),
            pltpu.SemaphoreType.DMA((2, 2)),
        ],
        compiler_params=pltpu.CompilerParams(collective_id=0, has_side_effects=True),
    )(rhs, labels, sigma_table.T)


def solution(mesh):
    placed = (P("groups", "slab", None, None), P("slab", "groups", None), P())
    return jax.shard_map(
        functools.partial(on_device, mesh.shape["slab"]),
        mesh=mesh,
        in_specs=placed,
        out_specs=P("groups", "slab", None, None),
        check_vma=False,
    )
```

```python
import functools

import jax
import jax.numpy as jnp
from jax import lax
from jax.experimental import pallas as pl
from jax.experimental.pallas import tpu as pltpu
from jax.sharding import PartitionSpec as P

OMEGA = 0.8
LABELS = 5
MESH = pl.DeviceIdType.MESH


def copy_to(src, dst, sems, slot, target):
    return pltpu.make_async_remote_copy(
        src_ref=src,
        dst_ref=dst,
        send_sem=sems.at[0, slot],
        recv_sem=sems.at[1, slot],
        device_id={"slab": target},
        device_id_type=MESH,
    )


def kernel(
    n, rhs_hbm, lab_hbm, table_hbm, out,
    lab, rhs, gx, gy, gzl, gzh, idf, dg, ua, ub, tmp, pro,
    cof, d1, b1, vn, line_out, line_all, row_out, row_all, xs, table,
    load_sem, sems, gather_sem,
):
    me = lax.axis_index("slab")
    nx, ny = lab.shape[1:]
    hx_rows = nx // 2
    has_low, has_up = me > 0, me < n - 1

    load_table = pltpu.make_async_copy(table_hbm, table, load_sem.at[2])
    load_table.start()
    barrier = pltpu.get_barrier_semaphore()

    def greet(step, carry):
        other = lax.rem(me + step, n)
        pl.semaphore_signal(barrier, inc=1, device_id={"slab": other}, device_id_type=MESH)
        return carry

    lax.fori_loop(1, n, greet, 0)
    pl.semaphore_wait(barrier, n - 1)

    up, low = lax.rem(me + 1, n), lax.rem(me + n - 1, n)
    near_up = copy_to(lab_hbm.at[3], lab.at[1], sems, 0, up)
    near_low = copy_to(lab_hbm.at[0], lab.at[6], sems, 1, low)
    next_up = copy_to(lab_hbm.at[2], lab.at[0], sems, 2, up)
    next_low = copy_to(lab_hbm.at[1], lab.at[7], sems, 3, low)
    rhs_up = copy_to(rhs_hbm.at[0, 3], rhs.at[1], sems, 4, up)
    rhs_low = copy_to(rhs_hbm.at[0, 0], rhs.at[6], sems, 5, low)
    u1_up = copy_to(ua.at[4], ua.at[0], sems, 6, up)
    u1_low = copy_to(ua.at[3], ua.at[7], sems, 7, low)
    cof_up = copy_to(cof.at[1, pl.ds(0, 4)], cof.at[0, pl.ds(0, 4)], sems, 8, up)
    cof_low = copy_to(cof.at[1, pl.ds(1, 4)], cof.at[2, pl.ds(1, 4)], sems, 9, low)
    b1_up = copy_to(b1.at[1], b1.at[0], sems, 10, up)
    b1_low = copy_to(b1.at[1], b1.at[2], sems, 11, low)
    u2_up = copy_to(ub.at[4], ub.at[0], sems, 12, up)
    u2_low = copy_to(ub.at[3], ub.at[7], sems, 13, low)
    vn_up = copy_to(vn.at[1], vn.at[0], sems, 14, up)
    vn_low = copy_to(vn.at[1], vn.at[2], sems, 15, low)

    def send(upward, downward):
        pl.when(has_up)(upward.start)
        pl.when(has_low)(downward.start)

    def receive(upward, downward):
        pl.when(has_low)(upward.wait_recv)
        pl.when(has_up)(downward.wait_recv)

    send(near_up, near_low)
    own_lab = pltpu.make_async_copy(lab_hbm, lab.at[pl.ds(2, 4)], load_sem.at[0])
    own_rhs = pltpu.make_async_copy(rhs_hbm.at[0], rhs.at[pl.ds(2, 4)], load_sem.at[1])
    own_lab.start()
    own_rhs.start()
    send(next_up, next_low)
    send(rhs_up, rhs_low)

    def clear(ref, first, count):
        for k in range(first, first + count):
            ref[k] = jnp.zeros(ref.shape[1:], ref.dtype)

    @pl.when(me == 0)
    def _():
        clear(lab, 0, 2)
        clear(rhs, 1, 1)
        clear(ua, 0, 1)
        clear(cof.at[0], 0, 4)
        clear(b1, 0, 1)
        clear(ub, 0, 1)
        clear(vn, 0, 1)

    @pl.when(me == n - 1)
    def _():
        clear(lab, 6, 2)
        clear(rhs, 6, 1)
        clear(ua, 7, 1)
        clear(cof.at[2], 1, 4)
        clear(b1, 2, 1)
        clear(ub, 7, 1)
        clear(vn, 2, 1)

    xs[...] = jnp.zeros(xs.shape, xs.dtype)

    fine_row = lax.broadcasted_iota(jnp.int32, (nx, ny), 0) % 2 == 1
    fine_lane = lax.broadcasted_iota(jnp.int32, (nx, ny), 1) % 2 == 1
    even = lax.broadcasted_iota(jnp.int32, (hx_rows, ny), 1) % 2 == 0

    def select(values, column):
        chosen = jnp.full(values.shape, table[column, 0], jnp.float32)
        for tissue in range(1, LABELS):
            chosen = jnp.where(values == tissue, table[column, tissue], chosen)
        return chosen

    def harmonic(a, b):
        return 2.0 * a * b / (a + b)

    def plane_terms(k):
        here, below, above = lab[k], lab[k - 1], lab[k + 1]
        a = (here > 0).astype(jnp.float32)
        sx, sy, sz = select(here, 0), select(here, 1), select(here, 2)
        hx = harmonic(pltpu.roll(sx, 1, 0), sx)
        faces = hx + pltpu.roll(hx, nx - 1, 0)
        cx = hx * a * pltpu.roll(a, 1, 0)
        gx[k] = cx
        hy = harmonic(pltpu.roll(sy, 1, 1), sy)
        faces = faces + hy + pltpu.roll(hy, ny - 1, 1)
        cy = hy * a * pltpu.roll(a, 1, 1)
        gy[k] = cy
        hl = harmonic(select(below, 2), sz)
        gzl[k] = hl * a * (below > 0).astype(jnp.float32)
        hh = harmonic(sz, select(above, 2))
        gzh[k] = hh * a * (above > 0).astype(jnp.float32)
        faces = faces + hl + hh
        diagonal = a * faces + (1.0 - a)
        dg[k] = diagonal
        idf[k] = OMEGA * a / diagonal

    def over(first, last, body):
        for k in range(first, last):
            body(k)

    def first_sweep(k):
        ua[k] = idf[k] * rhs[k]

    def neighbours(field, k):
        u = field[k]
        cx, cy = gx[k], gy[k]
        total = cx * pltpu.roll(u, 1, 0) + pltpu.roll(cx * u, nx - 1, 0)
        total = total + cy * pltpu.roll(u, 1, 1) + pltpu.roll(cy * u, ny - 1, 1)
        return u, total + gzl[k] * field[k - 1] + gzh[k] * field[k + 1]

    def sweep(src, dst, shift=0):
        def body(k):
            u, total = neighbours(src, k)
            dst[k - shift] = (1.0 - OMEGA) * u + idf[k] * (rhs[k] + total)

        return body

    def residual(k):
        u, total = neighbours(ub, k)
        return jnp.where(idf[k] > 0.0, rhs[k] - dg[k] * u + total, 0.0)

    second_sweep = sweep(ua, ub)

    load_table.wait()
    own_lab.wait()
    over(3, 5, plane_terms)
    own_rhs.wait()
    over(3, 5, first_sweep)
    send(u1_up, u1_low)

    receive(near_up, near_low)
    over(0, 2, lambda k: plane_terms(2 + 3 * k))
    over(0, 2, lambda k: first_sweep(2 + 3 * k))

    def rows_even(plane):
        tmp[0] = plane
        return tmp[0, pl.ds(0, hx_rows, 2), :]

    def rows_sum(plane):
        tmp[0] = plane
        return tmp[0, pl.ds(0, hx_rows, 2), :] + tmp[0, pl.ds(1, hx_rows, 2), :]

    def lanes_sum(t0, t1):
        return jnp.where(even, t0 + pltpu.roll(t0, ny - 1, 1), t1 + pltpu.roll(t1, 1, 1))

    def lanes_even(t0, t1):
        return jnp.where(even, t0, pltpu.roll(t1, 1, 1))

    def restrict(p0, p1):
        return lanes_sum(rows_sum(p0), rows_sum(p1))

    def inner(k):
        mask = (idf[k] > 0.0).astype(jnp.float32)
        doubled = jnp.where(fine_row, gx[k], 0.0) + jnp.where(fine_lane, gy[k], 0.0)
        if k % 2 == 1:
            doubled = doubled + gzl[k]
        return mask * dg[k] - 2.0 * doubled, mask

    (f0, m0), (f1, m1), (f2, m2), (f3, m3) = inner(2), inner(3), inner(4), inner(5)
    raw = restrict(f0 + f1, f2 + f3)
    active1 = jnp.minimum(restrict(m0 + m1, m2 + m3), 1.0)
    diag1 = raw + (1.0 - active1)
    d1[...] = diag1
    cof[1, 1] = OMEGA * active1 / diag1
    coarse_x = lanes_sum(rows_even(gx[2] + gx[3]), rows_even(gx[4] + gx[5]))
    coarse_y = lanes_even(rows_sum(gy[2] + gy[3]), rows_sum(gy[4] + gy[5]))
    coarse_zl = restrict(gzl[2], gzl[4])
    cof[1, 2] = coarse_x
    cof[1, 3] = coarse_y
    cof[1, 0] = coarse_zl
    cof[1, 4] = restrict(gzh[3], gzh[5])
    send(cof_up, cof_low)

    def plane_sums(packed):
        lower = jnp.sum(jnp.where(even, packed, 0.0), axis=0, keepdims=True)
        upper = jnp.sum(jnp.where(even, 0.0, packed), axis=0, keepdims=True)
        lower = jnp.sum(lower, axis=1, keepdims=True)
        upper = jnp.sum(upper, axis=1, keepdims=True)
        return lower, upper

    sub = lax.broadcasted_iota(jnp.int32, (8, ny), 0)

    sub_even = lax.broadcasted_iota(jnp.int32, (8, ny), 1) % 2 == 0

    def gather(out, everyone, slot, pairs):
        tile = jnp.zeros((8, ny), jnp.float32)
        for row, (lower, upper) in enumerate(pairs):
            tile = jnp.where(sub == row, jnp.where(sub_even, lower, upper), tile)
        out[...] = tile
        everyone[me] = tile
        rows = pl.ds(0, len(pairs))

        def one(step, carry):
            pltpu.make_async_remote_copy(
                src_ref=out.at[rows],
                dst_ref=everyone.at[me, rows],
                send_sem=gather_sem.at[0, slot],
                recv_sem=gather_sem.at[1, slot],
                device_id={"slab": lax.rem(me + step, n)},
                device_id_type=MESH,
            ).start()
            return carry

        lax.fori_loop(1, n, one, 0)

    def gather_wait(everyone, side, slot, count):
        rest = everyone.at[pl.ds(0, n - 1), pl.ds(0, count)]
        pltpu.make_async_copy(rest, rest, gather_sem.at[side, slot]).wait()

    line_diag = plane_sums(raw - 2.0 * (coarse_x + coarse_y))
    gather(line_out, line_all, 0, (line_diag, plane_sums(coarse_zl)))

    over(3, 5, second_sweep)
    receive(next_up, next_low)
    over(0, 2, lambda k: plane_terms(1 + 5 * k))
    receive(rhs_up, rhs_low)
    over(0, 2, lambda k: first_sweep(1 + 5 * k))
    over(0, 2, lambda k: second_sweep(2 + 3 * k))
    r3, r4 = residual(3), residual(4)
    receive(u1_up, u1_low)
    over(0, 2, lambda k: second_sweep(1 + 5 * k))
    b1[1] = restrict(residual(2) + r3, r4 + residual(5))
    send(b1_up, b1_low)
    send(u2_up, u2_low)

    gather_wait(line_all, 1, 0, 2)

    line_even = lax.broadcasted_iota(jnp.int32, (n, ny), 1) % 2 == 0

    def line_rows(everyone, row):
        both = everyone.reshape(n * 8, ny)[pl.ds(row, n, 8), :]
        lower = jnp.where(line_even, both, pltpu.roll(both, 1, 1))
        return lower, jnp.where(line_even, pltpu.roll(both, ny - 1, 1), both)

    (de, do), (fe, fo) = line_rows(line_all, 0), line_rows(line_all, 1)

    def back(x, s):
        return pltpu.roll(x, s % n, 0)

    def ahead(x, s):
        return pltpu.roll(x, (n - s) % n, 0)

    inv_odd = 1.0 / do
    to_low = fe * back(inv_odd, 1)
    to_up = fo * inv_odd
    fe_next = ahead(fe, 1)
    diag = de - fe * to_low - fo * to_up
    lower = -to_low * back(fo, 1)
    upper = -to_up * fe_next
    steps = []
    shift = 1
    while shift < n:
        alpha, gamma = lower / back(diag, shift), upper / ahead(diag, shift)
        steps.append((shift, alpha, gamma))
        diag = diag - alpha * back(upper, shift) - gamma * ahead(lower, shift)
        lower, upper = -alpha * back(lower, shift), -gamma * ahead(upper, shift)
        shift *= 2
    inv_diag = 1.0 / diag

    receive(cof_up, cof_low)
    cof[0, 4] = jnp.where(even, pltpu.roll(cof[0, 0], ny - 1, 1), pltpu.roll(cof[1, 0], 1, 1))
    cof[2, 0] = jnp.where(even, pltpu.roll(cof[1, 4], ny - 1, 1), pltpu.roll(cof[2, 4], 1, 1))
    receive(b1_up, b1_low)

    zero = jnp.zeros((hx_rows, ny), jnp.float32)

    def coarse_neighbours(k, below, f, above):
        cx, cy = cof[k, 2], cof[k, 3]
        zl = jnp.where(even, pltpu.roll(below, ny - 1, 1), pltpu.roll(f, 1, 1))
        zh = jnp.where(even, pltpu.roll(f, ny - 1, 1), pltpu.roll(above, 1, 1))
        total = cx * pltpu.roll(f, 1, 0)
        total = total + pltpu.roll(cx * f, hx_rows - 1, 0)
        total = total + cy * pltpu.roll(f, 2, 1)
        total = total + pltpu.roll(cy * f, ny - 2, 1)
        return total + cof[k, 0] * zl + cof[k, 4] * zh

    def coarse_sweep(fields):
        swept = []
        for k in range(3):
            total = coarse_neighbours(k, fields[k], fields[k + 1], fields[k + 2])
            swept.append((1.0 - OMEGA) * fields[k + 1] + cof[k, 1] * (b1[k] + total))
        return [zero] + swept + [zero]

    v1 = [zero] + [cof[k, 1] * b1[k] for k in range(3)] + [zero]
    v2 = coarse_sweep(v1)
    own_total = coarse_neighbours(1, v2[1], v2[2], v2[3])
    r1 = jnp.where(cof[1, 1] > 0.0, b1[1] - d1[...] * v2[2] + own_total, 0.0)
    gather(row_out, row_all, 1, (plane_sums(r1),))
    vn[1] = (1.0 - OMEGA) * v2[2] + cof[1, 1] * (b1[1] + own_total)
    send(vn_up, vn_low)

    parts = []
    for k in range(3):
        weight, cx, cy = cof[k, 1], cof[k, 2], cof[k, 3]
        around = cx + pltpu.roll(cx, hx_rows - 1, 0) + cy + pltpu.roll(cy, ny - 2, 1)
        own_part = jnp.where(weight > 0.0, 1.0 - OMEGA, 0.0) + weight * around
        parts.append((own_part, weight * cof[k, 0], weight * cof[k, 4]))
    receive(vn_up, vn_low)

    gather_wait(row_all, 1, 1, 1)
    be, bo = line_rows(row_all, 0)
    reduced = be + to_low * back(bo, 1) + to_up * bo
    for shift, alpha, gamma in steps:
        reduced = reduced - alpha * back(reduced, shift) - gamma * ahead(reduced, shift)
    e_even = reduced * inv_diag
    e_odd = (bo + fo * e_even + fe_next * ahead(e_even, 1)) * inv_odd
    packed = jnp.where(line_even, e_even, e_odd)
    xs[0, pl.ds(8, n), :] = packed
    xs[1, pl.ds(8, n), :] = jnp.where(line_even, back(e_odd, 1), e_even)
    xs[2, pl.ds(8, n), :] = jnp.where(line_even, e_odd, ahead(e_even, 1))

    def line(slot, k):
        return jnp.broadcast_to(xs[slot, pl.ds(me + 7 + k, 1), :], (hx_rows, ny))

    w2 = [zero]
    for k, (own_part, lower_part, upper_part) in enumerate(parts):
        fixed = own_part * line(0, k) + lower_part * line(1, k) + upper_part * line(2, k)
        w2.append(vn[k] + fixed)
    w3 = coarse_sweep(w2 + [zero])

    def prolong(slot, plane):
        pro[slot, pl.ds(0, hx_rows, 2), :] = plane
        pro[slot, pl.ds(1, hx_rows, 2), :] = plane

    def lower_plane(pack):
        return jnp.where(even, pack, pltpu.roll(pack, 1, 1))

    def upper_plane(pack):
        return jnp.where(even, pltpu.roll(pack, ny - 1, 1), pack)

    prolong(0, upper_plane(w3[1]))
    prolong(1, lower_plane(w3[2]))
    prolong(2, upper_plane(w3[2]))
    prolong(3, lower_plane(w3[3]))

    receive(u2_up, u2_low)

    def correct(k):
        ua[k] = ub[k] + jnp.where(lab[k] > 0, pro[k // 2], 0.0)

    pl.when(has_up)(u1_up.wait_send)
    pl.when(has_low)(u1_low.wait_send)
    over(0, 8, correct)

    over(1, 7, sweep(ua, tmp))
    over(2, 6, sweep(tmp, out.at[0], 2))

    for upward, downward in (
        (near_up, near_low), (next_up, next_low), (rhs_up, rhs_low), (cof_up, cof_low), (b1_up, b1_low), (vn_up, vn_low),
        (u2_up, u2_low),
    ):
        pl.when(has_up)(upward.wait_send)
        pl.when(has_low)(downward.wait_send)
    gather_wait(line_all, 0, 0, 2)
    gather_wait(row_all, 0, 1, 1)


def on_device(n, rhs, labels, sigma_table):
    planes, nx, ny = labels.shape
    fine = lambda count: pltpu.VMEM((count, nx, ny), jnp.float32)
    packs = lambda *counts: pltpu.VMEM((*counts, nx // 2, ny), jnp.float32)
    tiles = lambda *counts: pltpu.VMEM((*counts, 8, ny), jnp.float32)
    return pl.pallas_call(
        functools.partial(kernel, n),
        out_shape=pltpu.VMEM(rhs.shape, jnp.float32),
        in_specs=[
            pl.BlockSpec(memory_space=pl.ANY),
            pl.BlockSpec(memory_space=pl.ANY),
            pl.BlockSpec(memory_space=pl.ANY),
        ],
        out_specs=pl.BlockSpec(memory_space=pltpu.VMEM),
        scratch_shapes=[
            pltpu.VMEM((8, nx, ny), jnp.int32),
            fine(8), fine(8), fine(8), fine(8), fine(8), fine(8), fine(8), fine(8), fine(8),
            fine(8), fine(4),
            packs(3, 5), packs(), packs(3), packs(3),
            tiles(), tiles(n), tiles(), tiles(n),
            pltpu.VMEM((3, n + 16, ny), jnp.float32),
            pltpu.SMEM((3, LABELS), jnp.float32),
            pltpu.SemaphoreType.DMA((3,)),
            pltpu.SemaphoreType.DMA((2, 16)),
            pltpu.SemaphoreType.DMA((2, 2)),
        ],
        compiler_params=pltpu.CompilerParams(collective_id=0, has_side_effects=True),
    )(rhs, labels, sigma_table.T)


def solution(mesh):
    placed = (P("groups", "slab", None, None), P("slab", "groups", None), P())
    return jax.shard_map(
        functools.partial(on_device, mesh.shape["slab"]),
        mesh=mesh,
        in_specs=placed,
        out_specs=P("groups", "slab", None, None),
        check_vma=False,
    )
```

```python
import functools

import jax
import jax.numpy as jnp
from jax import lax
from jax.experimental import pallas as pl
from jax.experimental.pallas import tpu as pltpu
from jax.sharding import PartitionSpec as P

OMEGA = 0.8
LABELS = 5
MESH = pl.DeviceIdType.MESH


def copy_to(src, dst, sems, slot, target):
    return pltpu.make_async_remote_copy(
        src_ref=src,
        dst_ref=dst,
        send_sem=sems.at[0, slot],
        recv_sem=sems.at[1, slot],
        device_id={"slab": target},
        device_id_type=MESH,
    )


def kernel(
    n, rhs_hbm, lab_hbm, table_hbm, out,
    lab, rhs, gx, gy, gzl, gzh, idf, dg, ua, ub, tmp, pro,
    cof, d1, b1, vn, line_out, line_all, row_out, row_all, xs, table,
    load_sem, sems, gather_sem, tokens,
):
    me = lax.axis_index("slab")
    nx, ny = lab.shape[1:]
    hx_rows = nx // 2
    has_low, has_up = me > 0, me < n - 1

    load_table = pltpu.make_async_copy(table_hbm, table, load_sem.at[2])
    load_table.start()
    barrier = pltpu.get_barrier_semaphore()

    up, low = lax.rem(me + 1, n), lax.rem(me + n - 1, n)

    def greet(sem, distance):
        for near, other in ((me >= distance, me - distance), (me + distance < n, me + distance)):

            @pl.when(near)
            def _():
                pl.semaphore_signal(sem, inc=1, device_id={"slab": other}, device_id_type=MESH)

    def greeted(sem, distance):
        both = jnp.logical_and(me >= distance, me + distance < n)
        one = jnp.logical_xor(me >= distance, me + distance < n)
        pl.when(both)(lambda: pl.semaphore_wait(sem, 2))
        pl.when(one)(lambda: pl.semaphore_wait(sem, 1))

    greet(barrier, 1)
    greeted(barrier, 1)

    rounds = [2**r for r in range((n - 1).bit_length())]

    def round_start(r):
        if r < len(rounds):
            greet(tokens.at[r], rounds[r])

    def round_end(r):
        if r < len(rounds):
            greeted(tokens.at[r], rounds[r])

    near_up = copy_to(lab_hbm.at[3], lab.at[1], sems, 0, up)
    near_low = copy_to(lab_hbm.at[0], lab.at[6], sems, 1, low)
    next_up = copy_to(lab_hbm.at[2], lab.at[0], sems, 2, up)
    next_low = copy_to(lab_hbm.at[1], lab.at[7], sems, 3, low)
    rhs_up = copy_to(rhs_hbm.at[0, 3], rhs.at[1], sems, 4, up)
    rhs_low = copy_to(rhs_hbm.at[0, 0], rhs.at[6], sems, 5, low)
    u1_up = copy_to(ua.at[4], ua.at[0], sems, 6, up)
    u1_low = copy_to(ua.at[3], ua.at[7], sems, 7, low)
    cof_up = copy_to(cof.at[1, pl.ds(0, 4)], cof.at[0, pl.ds(0, 4)], sems, 8, up)
    cof_low = copy_to(cof.at[1, pl.ds(1, 4)], cof.at[2, pl.ds(1, 4)], sems, 9, low)
    b1_up = copy_to(b1.at[1], b1.at[0], sems, 10, up)
    b1_low = copy_to(b1.at[1], b1.at[2], sems, 11, low)
    u2_up = copy_to(ub.at[4], ub.at[0], sems, 12, up)
    u2_low = copy_to(ub.at[3], ub.at[7], sems, 13, low)
    vn_up = copy_to(vn.at[1], vn.at[0], sems, 14, up)
    vn_low = copy_to(vn.at[1], vn.at[2], sems, 15, low)

    def send(upward, downward):
        pl.when(has_up)(upward.start)
        pl.when(has_low)(downward.start)

    def receive(upward, downward):
        pl.when(has_low)(upward.wait_recv)
        pl.when(has_up)(downward.wait_recv)

    send(near_up, near_low)
    own_lab = pltpu.make_async_copy(lab_hbm, lab.at[pl.ds(2, 4)], load_sem.at[0])
    own_rhs = pltpu.make_async_copy(rhs_hbm.at[0], rhs.at[pl.ds(2, 4)], load_sem.at[1])
    own_lab.start()
    own_rhs.start()
    send(next_up, next_low)
    send(rhs_up, rhs_low)
    round_start(0)

    def clear(ref, first, count):
        for k in range(first, first + count):
            ref[k] = jnp.zeros(ref.shape[1:], ref.dtype)

    @pl.when(me == 0)
    def _():
        clear(lab, 0, 2)
        clear(rhs, 1, 1)
        clear(ua, 0, 1)
        clear(cof.at[0], 0, 4)
        clear(b1, 0, 1)
        clear(ub, 0, 1)
        clear(vn, 0, 1)

    @pl.when(me == n - 1)
    def _():
        clear(lab, 6, 2)
        clear(rhs, 6, 1)
        clear(ua, 7, 1)
        clear(cof.at[2], 1, 4)
        clear(b1, 2, 1)
        clear(ub, 7, 1)
        clear(vn, 2, 1)

    xs[...] = jnp.zeros(xs.shape, xs.dtype)

    fine_row = lax.broadcasted_iota(jnp.int32, (nx, ny), 0) % 2 == 1
    fine_lane = lax.broadcasted_iota(jnp.int32, (nx, ny), 1) % 2 == 1
    even = lax.broadcasted_iota(jnp.int32, (hx_rows, ny), 1) % 2 == 0

    def select(values, column):
        chosen = jnp.full(values.shape, table[column, 0], jnp.float32)
        for tissue in range(1, LABELS):
            chosen = jnp.where(values == tissue, table[column, tissue], chosen)
        return chosen

    def harmonic(a, b):
        return 2.0 * a * b / (a + b)

    def plane_terms(k):
        here, below, above = lab[k], lab[k - 1], lab[k + 1]
        a = (here > 0).astype(jnp.float32)
        sx, sy, sz = select(here, 0), select(here, 1), select(here, 2)
        hx = harmonic(pltpu.roll(sx, 1, 0), sx)
        faces = hx + pltpu.roll(hx, nx - 1, 0)
        cx = hx * a * pltpu.roll(a, 1, 0)
        gx[k] = cx
        hy = harmonic(pltpu.roll(sy, 1, 1), sy)
        faces = faces + hy + pltpu.roll(hy, ny - 1, 1)
        cy = hy * a * pltpu.roll(a, 1, 1)
        gy[k] = cy
        hl = harmonic(select(below, 2), sz)
        gzl[k] = hl * a * (below > 0).astype(jnp.float32)
        hh = harmonic(sz, select(above, 2))
        gzh[k] = hh * a * (above > 0).astype(jnp.float32)
        faces = faces + hl + hh
        diagonal = a * faces + (1.0 - a)
        dg[k] = diagonal
        idf[k] = OMEGA * a / diagonal

    def over(first, last, body):
        for k in range(first, last):
            body(k)

    def first_sweep(k):
        ua[k] = idf[k] * rhs[k]

    def neighbours(field, k):
        u = field[k]
        cx, cy = gx[k], gy[k]
        total = cx * pltpu.roll(u, 1, 0) + pltpu.roll(cx * u, nx - 1, 0)
        total = total + cy * pltpu.roll(u, 1, 1) + pltpu.roll(cy * u, ny - 1, 1)
        return u, total + gzl[k] * field[k - 1] + gzh[k] * field[k + 1]

    def sweep(src, dst, shift=0):
        def body(k):
            u, total = neighbours(src, k)
            dst[k - shift] = (1.0 - OMEGA) * u + idf[k] * (rhs[k] + total)

        return body

    def residual(k):
        u, total = neighbours(ub, k)
        return jnp.where(idf[k] > 0.0, rhs[k] - dg[k] * u + total, 0.0)

    second_sweep = sweep(ua, ub)

    load_table.wait()
    own_lab.wait()
    over(3, 5, plane_terms)
    own_rhs.wait()
    over(3, 5, first_sweep)
    send(u1_up, u1_low)

    receive(near_up, near_low)
    round_end(0)
    round_start(1)
    over(0, 2, lambda k: plane_terms(2 + 3 * k))
    over(0, 2, lambda k: first_sweep(2 + 3 * k))

    def rows_even(plane):
        tmp[0] = plane
        return tmp[0, pl.ds(0, hx_rows, 2), :]

    def rows_sum(plane):
        tmp[0] = plane
        return tmp[0, pl.ds(0, hx_rows, 2), :] + tmp[0, pl.ds(1, hx_rows, 2), :]

    def lanes_sum(t0, t1):
        return jnp.where(even, t0 + pltpu.roll(t0, ny - 1, 1), t1 + pltpu.roll(t1, 1, 1))

    def lanes_even(t0, t1):
        return jnp.where(even, t0, pltpu.roll(t1, 1, 1))

    def restrict(p0, p1):
        return lanes_sum(rows_sum(p0), rows_sum(p1))

    def inner(k):
        mask = (idf[k] > 0.0).astype(jnp.float32)
        doubled = jnp.where(fine_row, gx[k], 0.0) + jnp.where(fine_lane, gy[k], 0.0)
        if k % 2 == 1:
            doubled = doubled + gzl[k]
        return mask * dg[k] - 2.0 * doubled, mask

    (f0, m0), (f1, m1), (f2, m2), (f3, m3) = inner(2), inner(3), inner(4), inner(5)
    raw = restrict(f0 + f1, f2 + f3)
    active1 = jnp.minimum(restrict(m0 + m1, m2 + m3), 1.0)
    diag1 = raw + (1.0 - active1)
    d1[...] = diag1
    cof[1, 1] = OMEGA * active1 / diag1
    coarse_x = lanes_sum(rows_even(gx[2] + gx[3]), rows_even(gx[4] + gx[5]))
    coarse_y = lanes_even(rows_sum(gy[2] + gy[3]), rows_sum(gy[4] + gy[5]))
    coarse_zl = restrict(gzl[2], gzl[4])
    cof[1, 2] = coarse_x
    cof[1, 3] = coarse_y
    cof[1, 0] = coarse_zl
    cof[1, 4] = restrict(gzh[3], gzh[5])
    send(cof_up, cof_low)

    def plane_sums(packed):
        lower = jnp.sum(jnp.where(even, packed, 0.0), axis=0, keepdims=True)
        upper = jnp.sum(jnp.where(even, 0.0, packed), axis=0, keepdims=True)
        lower = jnp.sum(lower, axis=1, keepdims=True)
        upper = jnp.sum(upper, axis=1, keepdims=True)
        return lower, upper

    sub = lax.broadcasted_iota(jnp.int32, (8, ny), 0)

    sub_even = lax.broadcasted_iota(jnp.int32, (8, ny), 1) % 2 == 0

    def gather(out, everyone, slot, pairs):
        tile = jnp.zeros((8, ny), jnp.float32)
        for row, (lower, upper) in enumerate(pairs):
            tile = jnp.where(sub == row, jnp.where(sub_even, lower, upper), tile)
        out[...] = tile
        everyone[me] = tile
        rows = pl.ds(0, len(pairs))

        def one(step, carry):
            pltpu.make_async_remote_copy(
                src_ref=out.at[rows],
                dst_ref=everyone.at[me, rows],
                send_sem=gather_sem.at[0, slot],
                recv_sem=gather_sem.at[1, slot],
                device_id={"slab": lax.rem(me + step, n)},
                device_id_type=MESH,
            ).start()
            return carry

        lax.fori_loop(1, n, one, 0)

    def gather_wait(everyone, side, slot, count):
        rest = everyone.at[pl.ds(0, n - 1), pl.ds(0, count)]
        pltpu.make_async_copy(rest, rest, gather_sem.at[side, slot]).wait()

    line_diag = plane_sums(raw - 2.0 * (coarse_x + coarse_y))
    line_face = plane_sums(coarse_zl)

    over(3, 5, second_sweep)
    receive(next_up, next_low)
    round_end(1)
    round_start(2)
    over(0, 2, lambda k: plane_terms(1 + 5 * k))
    receive(rhs_up, rhs_low)
    round_end(2)
    round_start(3)
    over(0, 2, lambda k: first_sweep(1 + 5 * k))
    over(0, 2, lambda k: second_sweep(2 + 3 * k))
    r3, r4 = residual(3), residual(4)
    receive(u1_up, u1_low)
    over(0, 2, lambda k: second_sweep(1 + 5 * k))
    b1[1] = restrict(residual(2) + r3, r4 + residual(5))
    send(b1_up, b1_low)
    send(u2_up, u2_low)
    for r in range(3, len(rounds)):
        round_end(r)
        round_start(r + 1)
    gather(line_out, line_all, 0, (line_diag, line_face))

    receive(cof_up, cof_low)
    cof[0, 4] = jnp.where(even, pltpu.roll(cof[0, 0], ny - 1, 1), pltpu.roll(cof[1, 0], 1, 1))
    cof[2, 0] = jnp.where(even, pltpu.roll(cof[1, 4], ny - 1, 1), pltpu.roll(cof[2, 4], 1, 1))
    receive(b1_up, b1_low)

    zero = jnp.zeros((hx_rows, ny), jnp.float32)

    def coarse_neighbours(k, below, f, above):
        cx, cy = cof[k, 2], cof[k, 3]
        zl = jnp.where(even, pltpu.roll(below, ny - 1, 1), pltpu.roll(f, 1, 1))
        zh = jnp.where(even, pltpu.roll(f, ny - 1, 1), pltpu.roll(above, 1, 1))
        total = cx * pltpu.roll(f, 1, 0)
        total = total + pltpu.roll(cx * f, hx_rows - 1, 0)
        total = total + cy * pltpu.roll(f, 2, 1)
        total = total + pltpu.roll(cy * f, ny - 2, 1)
        return total + cof[k, 0] * zl + cof[k, 4] * zh

    def coarse_sweep(fields):
        swept = []
        for k in range(3):
            total = coarse_neighbours(k, fields[k], fields[k + 1], fields[k + 2])
            swept.append((1.0 - OMEGA) * fields[k + 1] + cof[k, 1] * (b1[k] + total))
        return [zero] + swept + [zero]

    v1 = [zero] + [cof[k, 1] * b1[k] for k in range(3)] + [zero]
    v2 = coarse_sweep(v1)
    own_total = coarse_neighbours(1, v2[1], v2[2], v2[3])
    r1 = jnp.where(cof[1, 1] > 0.0, b1[1] - d1[...] * v2[2] + own_total, 0.0)
    gather(row_out, row_all, 1, (plane_sums(r1),))
    vn[1] = (1.0 - OMEGA) * v2[2] + cof[1, 1] * (b1[1] + own_total)
    send(vn_up, vn_low)

    parts = []
    for k in range(3):
        weight, cx, cy = cof[k, 1], cof[k, 2], cof[k, 3]
        around = cx + pltpu.roll(cx, hx_rows - 1, 0) + cy + pltpu.roll(cy, ny - 2, 1)
        own_part = jnp.where(weight > 0.0, 1.0 - OMEGA, 0.0) + weight * around
        parts.append((own_part, weight * cof[k, 0], weight * cof[k, 4]))

    gather_wait(line_all, 1, 0, 2)

    line_even = lax.broadcasted_iota(jnp.int32, (n, ny), 1) % 2 == 0

    def line_rows(everyone, row):
        both = everyone.reshape(n * 8, ny)[pl.ds(row, n, 8), :]
        lower = jnp.where(line_even, both, pltpu.roll(both, 1, 1))
        return lower, jnp.where(line_even, pltpu.roll(both, ny - 1, 1), both)

    (de, do), (fe, fo) = line_rows(line_all, 0), line_rows(line_all, 1)

    def back(x, s):
        return pltpu.roll(x, s % n, 0)

    def ahead(x, s):
        return pltpu.roll(x, (n - s) % n, 0)

    inv_odd = 1.0 / do
    to_low = fe * back(inv_odd, 1)
    to_up = fo * inv_odd
    fe_next = ahead(fe, 1)
    diag = de - fe * to_low - fo * to_up
    lower = -to_low * back(fo, 1)
    upper = -to_up * fe_next
    steps = []
    shift = 1
    while shift < n:
        alpha, gamma = lower / back(diag, shift), upper / ahead(diag, shift)
        steps.append((shift, alpha, gamma))
        diag = diag - alpha * back(upper, shift) - gamma * ahead(lower, shift)
        lower, upper = -alpha * back(lower, shift), -gamma * ahead(upper, shift)
        shift *= 2
    inv_diag = 1.0 / diag

    receive(vn_up, vn_low)
    gather_wait(row_all, 1, 1, 1)
    be, bo = line_rows(row_all, 0)
    reduced = be + to_low * back(bo, 1) + to_up * bo
    for shift, alpha, gamma in steps:
        reduced = reduced - alpha * back(reduced, shift) - gamma * ahead(reduced, shift)
    e_even = reduced * inv_diag
    e_odd = (bo + fo * e_even + fe_next * ahead(e_even, 1)) * inv_odd
    packed = jnp.where(line_even, e_even, e_odd)
    xs[0, pl.ds(8, n), :] = packed
    xs[1, pl.ds(8, n), :] = jnp.where(line_even, back(e_odd, 1), e_even)
    xs[2, pl.ds(8, n), :] = jnp.where(line_even, e_odd, ahead(e_even, 1))

    def line(slot, k):
        return jnp.broadcast_to(xs[slot, pl.ds(me + 7 + k, 1), :], (hx_rows, ny))

    w2 = [zero]
    for k, (own_part, lower_part, upper_part) in enumerate(parts):
        fixed = own_part * line(0, k) + lower_part * line(1, k) + upper_part * line(2, k)
        w2.append(vn[k] + fixed)
    w3 = coarse_sweep(w2 + [zero])

    def prolong(slot, plane):
        pro[slot, pl.ds(0, hx_rows, 2), :] = plane
        pro[slot, pl.ds(1, hx_rows, 2), :] = plane

    def lower_plane(pack):
        return jnp.where(even, pack, pltpu.roll(pack, 1, 1))

    def upper_plane(pack):
        return jnp.where(even, pltpu.roll(pack, ny - 1, 1), pack)

    prolong(0, upper_plane(w3[1]))
    prolong(1, lower_plane(w3[2]))
    prolong(2, upper_plane(w3[2]))
    prolong(3, lower_plane(w3[3]))

    receive(u2_up, u2_low)

    def correct(k):
        ua[k] = ub[k] + jnp.where(lab[k] > 0, pro[k // 2], 0.0)

    pl.when(has_up)(u1_up.wait_send)
    pl.when(has_low)(u1_low.wait_send)
    over(0, 8, correct)

    over(1, 7, sweep(ua, tmp))
    over(2, 6, sweep(tmp, out.at[0], 2))

    for upward, downward in (
        (near_up, near_low), (next_up, next_low), (rhs_up, rhs_low), (cof_up, cof_low), (b1_up, b1_low), (vn_up, vn_low),
        (u2_up, u2_low),
    ):
        pl.when(has_up)(upward.wait_send)
        pl.when(has_low)(downward.wait_send)
    gather_wait(line_all, 0, 0, 2)
    gather_wait(row_all, 0, 1, 1)


def on_device(n, rhs, labels, sigma_table):
    planes, nx, ny = labels.shape
    fine = lambda count: pltpu.VMEM((count, nx, ny), jnp.float32)
    packs = lambda *counts: pltpu.VMEM((*counts, nx // 2, ny), jnp.float32)
    tiles = lambda *counts: pltpu.VMEM((*counts, 8, ny), jnp.float32)
    return pl.pallas_call(
        functools.partial(kernel, n),
        out_shape=pltpu.VMEM(rhs.shape, jnp.float32),
        in_specs=[
            pl.BlockSpec(memory_space=pl.ANY),
            pl.BlockSpec(memory_space=pl.ANY),
            pl.BlockSpec(memory_space=pl.ANY),
        ],
        out_specs=pl.BlockSpec(memory_space=pltpu.VMEM),
        scratch_shapes=[
            pltpu.VMEM((8, nx, ny), jnp.int32),
            fine(8), fine(8), fine(8), fine(8), fine(8), fine(8), fine(8), fine(8), fine(8),
            fine(8), fine(4),
            packs(3, 5), packs(), packs(3), packs(3),
            tiles(), tiles(n), tiles(), tiles(n),
            pltpu.VMEM((3, n + 16, ny), jnp.float32),
            pltpu.SMEM((3, LABELS), jnp.float32),
            pltpu.SemaphoreType.DMA((3,)),
            pltpu.SemaphoreType.DMA((2, 16)),
            pltpu.SemaphoreType.DMA((2, 2)),
            pltpu.SemaphoreType.REGULAR((n.bit_length(),)),
        ],
        compiler_params=pltpu.CompilerParams(collective_id=0, has_side_effects=True),
    )(rhs, labels, sigma_table.T)


def solution(mesh):
    placed = (P("groups", "slab", None, None), P("slab", "groups", None), P())
    return jax.shard_map(
        functools.partial(on_device, mesh.shape["slab"]),
        mesh=mesh,
        in_specs=placed,
        out_specs=P("groups", "slab", None, None),
        check_vma=False,
    )
```

```python
import functools

import jax
import jax.numpy as jnp
from jax import lax
from jax.experimental import pallas as pl
from jax.experimental.pallas import tpu as pltpu
from jax.sharding import PartitionSpec as P

OMEGA = 0.8
LABELS = 5
MESH = pl.DeviceIdType.MESH


def copy_to(src, dst, sems, slot, target):
    return pltpu.make_async_remote_copy(
        src_ref=src,
        dst_ref=dst,
        send_sem=sems.at[0, slot],
        recv_sem=sems.at[1, slot],
        device_id={"slab": target},
        device_id_type=MESH,
    )


def kernel(
    n, rhs_hbm, lab_hbm, table_hbm, out,
    lab, rhs, gx, gy, gzl, gzh, idf, dg, ua, ub, tmp, pro,
    cof, d1, b1, vn, line_out, line_all, row_out, row_all, xs, table,
    load_sem, sems, gather_sem, tokens,
):
    me = lax.axis_index("slab")
    nx, ny = lab.shape[1:]
    hx_rows = nx // 2
    has_low, has_up = me > 0, me < n - 1

    load_table = pltpu.make_async_copy(table_hbm, table, load_sem.at[2])
    load_table.start()
    barrier = pltpu.get_barrier_semaphore()

    up, low = lax.rem(me + 1, n), lax.rem(me + n - 1, n)

    def greet(sem, distance):
        for near, other in ((me >= distance, me - distance), (me + distance < n, me + distance)):

            @pl.when(near)
            def _():
                pl.semaphore_signal(sem, inc=1, device_id={"slab": other}, device_id_type=MESH)

    def greeted(sem, distance):
        both = jnp.logical_and(me >= distance, me + distance < n)
        one = jnp.logical_xor(me >= distance, me + distance < n)
        pl.when(both)(lambda: pl.semaphore_wait(sem, 2))
        pl.when(one)(lambda: pl.semaphore_wait(sem, 1))

    greet(barrier, 1)
    greeted(barrier, 1)

    rounds = [2**r for r in range((n - 1).bit_length())]

    def round_start(r):
        if r < len(rounds):
            greet(tokens.at[r], rounds[r])

    def round_end(r):
        if r < len(rounds):
            greeted(tokens.at[r], rounds[r])

    near_up = copy_to(lab_hbm.at[3], lab.at[1], sems, 0, up)
    near_low = copy_to(lab_hbm.at[0], lab.at[6], sems, 1, low)
    next_up = copy_to(lab_hbm.at[2], lab.at[0], sems, 2, up)
    next_low = copy_to(lab_hbm.at[1], lab.at[7], sems, 3, low)
    rhs_up = copy_to(rhs_hbm.at[0, 3], rhs.at[1], sems, 4, up)
    rhs_low = copy_to(rhs_hbm.at[0, 0], rhs.at[6], sems, 5, low)
    u1_up = copy_to(ua.at[4], ua.at[0], sems, 6, up)
    u1_low = copy_to(ua.at[3], ua.at[7], sems, 7, low)
    cof_up = copy_to(cof.at[1, pl.ds(0, 4)], cof.at[0, pl.ds(0, 4)], sems, 8, up)
    cof_low = copy_to(cof.at[1, pl.ds(1, 4)], cof.at[2, pl.ds(1, 4)], sems, 9, low)
    b1_up = copy_to(b1.at[1], b1.at[0], sems, 10, up)
    b1_low = copy_to(b1.at[1], b1.at[2], sems, 11, low)
    u2_up = copy_to(ub.at[4], ub.at[0], sems, 12, up)
    u2_low = copy_to(ub.at[3], ub.at[7], sems, 13, low)
    vn_up = copy_to(vn.at[1], vn.at[0], sems, 14, up)
    vn_low = copy_to(vn.at[1], vn.at[2], sems, 15, low)

    def send(upward, downward):
        pl.when(has_up)(upward.start)
        pl.when(has_low)(downward.start)

    def receive(upward, downward):
        pl.when(has_low)(upward.wait_recv)
        pl.when(has_up)(downward.wait_recv)

    send(near_up, near_low)
    own_lab = pltpu.make_async_copy(lab_hbm, lab.at[pl.ds(2, 4)], load_sem.at[0])
    own_rhs = pltpu.make_async_copy(rhs_hbm.at[0], rhs.at[pl.ds(2, 4)], load_sem.at[1])
    own_lab.start()
    own_rhs.start()
    send(next_up, next_low)
    send(rhs_up, rhs_low)
    round_start(0)

    def clear(ref, first, count):
        for k in range(first, first + count):
            ref[k] = jnp.zeros(ref.shape[1:], ref.dtype)

    @pl.when(me == 0)
    def _():
        clear(lab, 0, 2)
        clear(rhs, 1, 1)
        clear(ua, 0, 1)
        clear(cof.at[0], 0, 4)
        clear(b1, 0, 1)
        clear(ub, 0, 1)
        clear(vn, 0, 1)

    @pl.when(me == n - 1)
    def _():
        clear(lab, 6, 2)
        clear(rhs, 6, 1)
        clear(ua, 7, 1)
        clear(cof.at[2], 1, 4)
        clear(b1, 2, 1)
        clear(ub, 7, 1)
        clear(vn, 2, 1)

    xs[...] = jnp.zeros(xs.shape, xs.dtype)

    fine_row = lax.broadcasted_iota(jnp.int32, (nx, ny), 0) % 2 == 1
    fine_lane = lax.broadcasted_iota(jnp.int32, (nx, ny), 1) % 2 == 1
    even = lax.broadcasted_iota(jnp.int32, (hx_rows, ny), 1) % 2 == 0

    def select(values, column):
        chosen = jnp.full(values.shape, table[column, 0], jnp.float32)
        for tissue in range(1, LABELS):
            chosen = jnp.where(values == tissue, table[column, tissue], chosen)
        return chosen

    def harmonic(a, b):
        return 2.0 * a * b / (a + b)

    def plane_terms(k):
        here, below, above = lab[k], lab[k - 1], lab[k + 1]
        a = (here > 0).astype(jnp.float32)
        sx, sy, sz = select(here, 0), select(here, 1), select(here, 2)
        hx = harmonic(pltpu.roll(sx, 1, 0), sx)
        faces = hx + pltpu.roll(hx, nx - 1, 0)
        cx = hx * a * pltpu.roll(a, 1, 0)
        gx[k] = cx
        hy = harmonic(pltpu.roll(sy, 1, 1), sy)
        faces = faces + hy + pltpu.roll(hy, ny - 1, 1)
        cy = hy * a * pltpu.roll(a, 1, 1)
        gy[k] = cy
        hl = harmonic(select(below, 2), sz)
        gzl[k] = hl * a * (below > 0).astype(jnp.float32)
        hh = harmonic(sz, select(above, 2))
        gzh[k] = hh * a * (above > 0).astype(jnp.float32)
        faces = faces + hl + hh
        diagonal = a * faces + (1.0 - a)
        dg[k] = diagonal
        idf[k] = OMEGA * a / diagonal

    def over(first, last, body):
        for k in range(first, last):
            body(k)

    def first_sweep(k):
        ua[k] = idf[k] * rhs[k]

    def neighbours(field, k):
        u = field[k]
        cx, cy = gx[k], gy[k]
        total = cx * pltpu.roll(u, 1, 0) + pltpu.roll(cx * u, nx - 1, 0)
        total = total + cy * pltpu.roll(u, 1, 1) + pltpu.roll(cy * u, ny - 1, 1)
        return u, total + gzl[k] * field[k - 1] + gzh[k] * field[k + 1]

    def sweep(src, dst, shift=0):
        def body(k):
            u, total = neighbours(src, k)
            dst[k - shift] = (1.0 - OMEGA) * u + idf[k] * (rhs[k] + total)

        return body

    def residual(k):
        u, total = neighbours(ub, k)
        return jnp.where(idf[k] > 0.0, rhs[k] - dg[k] * u + total, 0.0)

    second_sweep = sweep(ua, ub)

    load_table.wait()
    own_lab.wait()
    over(3, 5, plane_terms)
    own_rhs.wait()
    over(3, 5, first_sweep)
    send(u1_up, u1_low)

    receive(near_up, near_low)
    round_end(0)
    round_start(1)
    over(0, 2, lambda k: plane_terms(2 + 3 * k))
    over(0, 2, lambda k: first_sweep(2 + 3 * k))

    def rows_even(plane):
        tmp[0] = plane
        return tmp[0, pl.ds(0, hx_rows, 2), :]

    def rows_sum(plane):
        tmp[0] = plane
        return tmp[0, pl.ds(0, hx_rows, 2), :] + tmp[0, pl.ds(1, hx_rows, 2), :]

    def lanes_sum(t0, t1):
        return jnp.where(even, t0 + pltpu.roll(t0, ny - 1, 1), t1 + pltpu.roll(t1, 1, 1))

    def lanes_even(t0, t1):
        return jnp.where(even, t0, pltpu.roll(t1, 1, 1))

    def restrict(p0, p1):
        return lanes_sum(rows_sum(p0), rows_sum(p1))

    def inner(k):
        mask = (idf[k] > 0.0).astype(jnp.float32)
        doubled = jnp.where(fine_row, gx[k], 0.0) + jnp.where(fine_lane, gy[k], 0.0)
        if k % 2 == 1:
            doubled = doubled + gzl[k]
        return mask * dg[k] - 2.0 * doubled, mask

    (f0, m0), (f1, m1), (f2, m2), (f3, m3) = inner(2), inner(3), inner(4), inner(5)
    raw = restrict(f0 + f1, f2 + f3)
    active1 = jnp.minimum(restrict(m0 + m1, m2 + m3), 1.0)
    diag1 = raw + (1.0 - active1)
    d1[...] = diag1
    cof[1, 1] = OMEGA * active1 / diag1
    coarse_x = lanes_sum(rows_even(gx[2] + gx[3]), rows_even(gx[4] + gx[5]))
    coarse_y = lanes_even(rows_sum(gy[2] + gy[3]), rows_sum(gy[4] + gy[5]))
    coarse_zl = restrict(gzl[2], gzl[4])
    cof[1, 2] = coarse_x
    cof[1, 3] = coarse_y
    cof[1, 0] = coarse_zl
    cof[1, 4] = restrict(gzh[3], gzh[5])
    send(cof_up, cof_low)

    def plane_sums(packed):
        lower = jnp.sum(jnp.where(even, packed, 0.0), axis=0, keepdims=True)
        upper = jnp.sum(jnp.where(even, 0.0, packed), axis=0, keepdims=True)
        lower = jnp.sum(lower, axis=1, keepdims=True)
        upper = jnp.sum(upper, axis=1, keepdims=True)
        return lower, upper

    sub = lax.broadcasted_iota(jnp.int32, (8, ny), 0)

    sub_even = lax.broadcasted_iota(jnp.int32, (8, ny), 1) % 2 == 0

    def gather(out, everyone, slot, pairs):
        tile = jnp.zeros((8, ny), jnp.float32)
        for row, (lower, upper) in enumerate(pairs):
            tile = jnp.where(sub == row, jnp.where(sub_even, lower, upper), tile)
        out[...] = tile
        everyone[me] = tile
        rows = pl.ds(0, len(pairs))

        def one(step, carry):
            pltpu.make_async_remote_copy(
                src_ref=out.at[rows],
                dst_ref=everyone.at[me, rows],
                send_sem=gather_sem.at[0, slot],
                recv_sem=gather_sem.at[1, slot],
                device_id={"slab": lax.rem(me + step, n)},
                device_id_type=MESH,
            ).start()
            return carry

        lax.fori_loop(1, n, one, 0)

    def gather_wait(everyone, side, slot, count):
        rest = everyone.at[pl.ds(0, n - 1), pl.ds(0, count)]
        pltpu.make_async_copy(rest, rest, gather_sem.at[side, slot]).wait()

    line_diag = plane_sums(raw - 2.0 * (coarse_x + coarse_y))
    line_face = plane_sums(coarse_zl)

    over(3, 5, second_sweep)
    receive(next_up, next_low)
    round_end(1)
    round_start(2)
    over(0, 2, lambda k: plane_terms(1 + 5 * k))
    receive(rhs_up, rhs_low)
    round_end(2)
    round_start(3)
    over(0, 2, lambda k: first_sweep(1 + 5 * k))
    over(0, 2, lambda k: second_sweep(2 + 3 * k))
    r3, r4 = residual(3), residual(4)
    receive(u1_up, u1_low)
    over(0, 2, lambda k: second_sweep(1 + 5 * k))
    b1[1] = restrict(residual(2) + r3, r4 + residual(5))
    send(b1_up, b1_low)
    for r in range(3, len(rounds)):
        round_end(r)
        round_start(r + 1)
    gather(line_out, line_all, 0, (line_diag, line_face))
    send(u2_up, u2_low)

    receive(cof_up, cof_low)
    cof[0, 4] = jnp.where(even, pltpu.roll(cof[0, 0], ny - 1, 1), pltpu.roll(cof[1, 0], 1, 1))
    cof[2, 0] = jnp.where(even, pltpu.roll(cof[1, 4], ny - 1, 1), pltpu.roll(cof[2, 4], 1, 1))
    receive(b1_up, b1_low)

    zero = jnp.zeros((hx_rows, ny), jnp.float32)

    def coarse_neighbours(k, below, f, above):
        cx, cy = cof[k, 2], cof[k, 3]
        zl = jnp.where(even, pltpu.roll(below, ny - 1, 1), pltpu.roll(f, 1, 1))
        zh = jnp.where(even, pltpu.roll(f, ny - 1, 1), pltpu.roll(above, 1, 1))
        total = cx * pltpu.roll(f, 1, 0)
        total = total + pltpu.roll(cx * f, hx_rows - 1, 0)
        total = total + cy * pltpu.roll(f, 2, 1)
        total = total + pltpu.roll(cy * f, ny - 2, 1)
        return total + cof[k, 0] * zl + cof[k, 4] * zh

    def coarse_sweep(fields):
        swept = []
        for k in range(3):
            total = coarse_neighbours(k, fields[k], fields[k + 1], fields[k + 2])
            swept.append((1.0 - OMEGA) * fields[k + 1] + cof[k, 1] * (b1[k] + total))
        return [zero] + swept + [zero]

    v1 = [zero] + [cof[k, 1] * b1[k] for k in range(3)] + [zero]
    v2 = coarse_sweep(v1)
    own_total = coarse_neighbours(1, v2[1], v2[2], v2[3])
    r1 = jnp.where(cof[1, 1] > 0.0, b1[1] - d1[...] * v2[2] + own_total, 0.0)
    gather(row_out, row_all, 1, (plane_sums(r1),))
    vn[1] = (1.0 - OMEGA) * v2[2] + cof[1, 1] * (b1[1] + own_total)
    send(vn_up, vn_low)

    parts = []
    for k in range(3):
        weight, cx, cy = cof[k, 1], cof[k, 2], cof[k, 3]
        around = cx + pltpu.roll(cx, hx_rows - 1, 0) + cy + pltpu.roll(cy, ny - 2, 1)
        own_part = jnp.where(weight > 0.0, 1.0 - OMEGA, 0.0) + weight * around
        parts.append((own_part, weight * cof[k, 0], weight * cof[k, 4]))

    gather_wait(line_all, 1, 0, 2)

    line_even = lax.broadcasted_iota(jnp.int32, (n, ny), 1) % 2 == 0

    def line_rows(everyone, row):
        both = everyone.reshape(n * 8, ny)[pl.ds(row, n, 8), :]
        lower = jnp.where(line_even, both, pltpu.roll(both, 1, 1))
        return lower, jnp.where(line_even, pltpu.roll(both, ny - 1, 1), both)

    (de, do), (fe, fo) = line_rows(line_all, 0), line_rows(line_all, 1)

    def back(x, s):
        return pltpu.roll(x, s % n, 0)

    def ahead(x, s):
        return pltpu.roll(x, (n - s) % n, 0)

    inv_odd = 1.0 / do
    to_low = fe * back(inv_odd, 1)
    to_up = fo * inv_odd
    fe_next = ahead(fe, 1)
    diag = de - fe * to_low - fo * to_up
    lower = -to_low * back(fo, 1)
    upper = -to_up * fe_next
    steps = []
    shift = 1
    while shift < n:
        alpha, gamma = lower / back(diag, shift), upper / ahead(diag, shift)
        steps.append((shift, alpha, gamma))
        diag = diag - alpha * back(upper, shift) - gamma * ahead(lower, shift)
        lower, upper = -alpha * back(lower, shift), -gamma * ahead(upper, shift)
        shift *= 2
    inv_diag = 1.0 / diag

    receive(vn_up, vn_low)
    gather_wait(row_all, 1, 1, 1)
    be, bo = line_rows(row_all, 0)
    reduced = be + to_low * back(bo, 1) + to_up * bo
    for shift, alpha, gamma in steps:
        reduced = reduced - alpha * back(reduced, shift) - gamma * ahead(reduced, shift)
    e_even = reduced * inv_diag
    e_odd = (bo + fo * e_even + fe_next * ahead(e_even, 1)) * inv_odd
    packed = jnp.where(line_even, e_even, e_odd)
    xs[0, pl.ds(8, n), :] = packed
    xs[1, pl.ds(8, n), :] = jnp.where(line_even, back(e_odd, 1), e_even)
    xs[2, pl.ds(8, n), :] = jnp.where(line_even, e_odd, ahead(e_even, 1))

    def line(slot, k):
        return jnp.broadcast_to(xs[slot, pl.ds(me + 7 + k, 1), :], (hx_rows, ny))

    w2 = [zero]
    for k, (own_part, lower_part, upper_part) in enumerate(parts):
        fixed = own_part * line(0, k) + lower_part * line(1, k) + upper_part * line(2, k)
        w2.append(vn[k] + fixed)
    w3 = coarse_sweep(w2 + [zero])

    def prolong(slot, plane):
        pro[slot, pl.ds(0, hx_rows, 2), :] = plane
        pro[slot, pl.ds(1, hx_rows, 2), :] = plane

    def lower_plane(pack):
        return jnp.where(even, pack, pltpu.roll(pack, 1, 1))

    def upper_plane(pack):
        return jnp.where(even, pltpu.roll(pack, ny - 1, 1), pack)

    prolong(0, upper_plane(w3[1]))
    prolong(1, lower_plane(w3[2]))
    prolong(2, upper_plane(w3[2]))
    prolong(3, lower_plane(w3[3]))

    receive(u2_up, u2_low)

    def correct(k):
        ua[k] = ub[k] + jnp.where(lab[k] > 0, pro[k // 2], 0.0)

    pl.when(has_up)(u1_up.wait_send)
    pl.when(has_low)(u1_low.wait_send)
    over(0, 8, correct)

    over(1, 7, sweep(ua, tmp))
    over(2, 6, sweep(tmp, out.at[0], 2))

    for upward, downward in (
        (near_up, near_low), (next_up, next_low), (rhs_up, rhs_low), (cof_up, cof_low), (b1_up, b1_low), (vn_up, vn_low),
        (u2_up, u2_low),
    ):
        pl.when(has_up)(upward.wait_send)
        pl.when(has_low)(downward.wait_send)
    gather_wait(line_all, 0, 0, 2)
    gather_wait(row_all, 0, 1, 1)


def on_device(n, rhs, labels, sigma_table):
    planes, nx, ny = labels.shape
    fine = lambda count: pltpu.VMEM((count, nx, ny), jnp.float32)
    packs = lambda *counts: pltpu.VMEM((*counts, nx // 2, ny), jnp.float32)
    tiles = lambda *counts: pltpu.VMEM((*counts, 8, ny), jnp.float32)
    return pl.pallas_call(
        functools.partial(kernel, n),
        out_shape=pltpu.VMEM(rhs.shape, jnp.float32),
        in_specs=[
            pl.BlockSpec(memory_space=pl.ANY),
            pl.BlockSpec(memory_space=pl.ANY),
            pl.BlockSpec(memory_space=pl.ANY),
        ],
        out_specs=pl.BlockSpec(memory_space=pltpu.VMEM),
        scratch_shapes=[
            pltpu.VMEM((8, nx, ny), jnp.int32),
            fine(8), fine(8), fine(8), fine(8), fine(8), fine(8), fine(8), fine(8), fine(8),
            fine(8), fine(4),
            packs(3, 5), packs(), packs(3), packs(3),
            tiles(), tiles(n), tiles(), tiles(n),
            pltpu.VMEM((3, n + 16, ny), jnp.float32),
            pltpu.SMEM((3, LABELS), jnp.float32),
            pltpu.SemaphoreType.DMA((3,)),
            pltpu.SemaphoreType.DMA((2, 16)),
            pltpu.SemaphoreType.DMA((2, 2)),
            pltpu.SemaphoreType.REGULAR((n.bit_length(),)),
        ],
        compiler_params=pltpu.CompilerParams(collective_id=0, has_side_effects=True),
    )(rhs, labels, sigma_table.T)


def solution(mesh):
    placed = (P("groups", "slab", None, None), P("slab", "groups", None), P())
    return jax.shard_map(
        functools.partial(on_device, mesh.shape["slab"]),
        mesh=mesh,
        in_specs=placed,
        out_specs=P("groups", "slab", None, None),
        check_vma=False,
    )
```
